256 devices in a mesh: gx: 64 (over z, x, core), gy: 4 (over y).
Axes of the slice: x: 4, y: 4, z: 8, core: 2. Of those that a mesh axis runs over, the one named last changes fastest.
Arguments:
- particles: float32 [4, 7, 393216], P('gy', None, 'gx'), may hold values from -4 to 1024, as said below
- routing: int32 [4, 2, 393216], P('gy', None, 'gx'), may hold values from 0 to 32767, as said below
- tile_list: int32 [4, 2, 409600], P('gy', None, 'gx'), may hold values from 0 to 400, as said below
Outputs:
- particle_rates: float32 [4, 4, 393216], P('gy', None, 'gx')
The draws below stay inside these ranges and needn't reach their ends.
Inputs may be any that keep to these rules, and one draw needn't show every extreme that they name: `routing`: row 0 is the new owner's gx index (the gy index does not change), row 1 the slot there. Each device's columns are grouped by new owner in increasing order. At most 192 of one device's particles go to one owner, and in every draw some owner receives exactly 192 from every device. No two particles share an owner and a slot. An owner's particles fill whole pencils, each from its first slot, all but one pencil at most. `particles`: positions lie in the cell of the particle's slot: pencil (i, j) covers [i, i + 1) x [j, j + 1) in x and y, cell k of a pencil, k = (slot % 128) // 8, covers [k, k + 1) in z. Masses are positive. `tile_list`: row 0 is a pencil a of the device, index i * 16 + j for local pencil (i, j); row 1 a pencil b, index (i + 2) * 20 + j + 2 for local pencil (i, j) counted from two pencils before the block, or 400 for an unused entry. The used entries come first in no fixed order, and are exactly the pairs in which both a and b hold particles and b is at most two pencils from a along x and along y. Unused entries have a = 0.
All inputs are finite; a program needn't handle non-finite values.
Results may differ from the reference program's by a relative error of at most 0.0003.
Values sent between devices are 32-bit elements; how exact they have to be, the bound alone decides.
A program may use at most 128 MiB of HBM per device.

```python
import math
import jax
import jax.numpy as jnp
from jax import lax

CX = 16
CY = 16
NZ = 16
CAP = 8
PART_DEV = 6144
N_GX = 64
N_GY = 4


def shared_layout(key):
    pencil_slots = NZ * CAP
    pencils = CX * CY
    capacity = 2 * PART_DEV // N_GX
    half_lanes = N_GX // 2
    order_keys = jax.random.split(jax.random.fold_in(key, 101), N_GY)
    orders = jax.vmap(lambda sub_key: jax.random.permutation(sub_key, N_GX))(order_keys).astype(jnp.int32)
    busy_ids = orders[:, 0::2]
    light_ids = orders[:, 1::2]
    spare = jax.random.randint(jax.random.fold_in(key, 102), (N_GY, N_GX, half_lanes), 0, capacity // 4 + 1).astype(jnp.int32)
    spare = spare.at[:, :, 0].set(0)
    owner_ids = jnp.arange(N_GX, dtype=jnp.int32)
    busy_hot = (busy_ids[:, :, None] == owner_ids[None, None, :]).astype(jnp.int32)
    light_hot = (light_ids[:, :, None] == owner_ids[None, None, :]).astype(jnp.int32)
    sends = jnp.sum((capacity - spare)[:, :, :, None] * busy_hot[:, None, :, :] + spare[:, :, :, None] * light_hot[:, None, :, :], axis=2).astype(jnp.int32)
    send_ends = jnp.cumsum(sends, axis=2).astype(jnp.int32)
    starts = send_ends - sends
    before = (jnp.cumsum(sends, axis=1) - sends).astype(jnp.int32)
    row_ids = jnp.arange(PART_DEV, dtype=jnp.int32)
    dest_ids = jax.vmap(jax.vmap(lambda edge_list: jnp.searchsorted(edge_list, row_ids, side='right')))(send_ends).astype(jnp.int32)
    offset = jnp.take_along_axis(before, dest_ids, axis=2) + row_ids[None, None, :] - jnp.take_along_axis(starts, dest_ids, axis=2)
    perm_keys = jax.random.split(jax.random.fold_in(key, 103), N_GY * N_GX)
    base_order = jax.vmap(lambda sub_key: jax.random.permutation(sub_key, pencils))(perm_keys).astype(jnp.int32)
    base_order = base_order.reshape(N_GY, N_GX, pencils)
    positions = jnp.arange(pencils, dtype=jnp.int32)
    lead_key = jnp.where(base_order == pencils - 1, -2, jnp.where(base_order == 0, -1, positions[None, None, :]))
    lead_order = jnp.argsort(lead_key, axis=2, stable=True)
    leading = jnp.take_along_axis(base_order, lead_order, axis=2)
    special = owner_ids[None, :] == busy_ids[:, 0:1]
    pencil_order = jnp.where(special[:, :, None], leading, base_order)
    row_axis = jnp.arange(N_GY, dtype=jnp.int32)[:, None, None]
    pencil_of = pencil_order[row_axis, dest_ids, offset // pencil_slots]
    slot_ids = pencil_of * pencil_slots + offset % pencil_slots
    received = before[:, -1, :] + sends[:, -1, :]
    filled = (received + pencil_slots - 1) // pencil_slots
    pencil_rank = jnp.argsort(pencil_order, axis=2, stable=True)
    occupied = pencil_rank < filled[:, :, None]
    return (dest_ids, slot_ids, occupied)


def draw_routing(key, part):
    dest_ids, slot_ids, occupied = shared_layout(key)
    stacked = jnp.stack([dest_ids, slot_ids], axis=1)
    return stacked.reshape(N_GY, 2, N_GX * PART_DEV).astype(jnp.int32)


def draw_tile_list(key, part):
    dest_ids, slot_ids, occupied = shared_layout(key)
    pencils = CX * CY
    ext_count = (CX + 4) * (CY + 4)
    npair = 25 * pencils
    global_occ = occupied.reshape(N_GY, N_GX, CX, CY).transpose(1, 2, 0, 3).reshape(N_GX * CX, N_GY * CY)
    padded = jnp.pad(global_occ, 2)
    lane_g = jnp.arange(N_GY, dtype=jnp.int32)[:, None, None, None, None, None]
    lane_d = jnp.arange(N_GX, dtype=jnp.int32)[None, :, None, None, None, None]
    pencil_x = jnp.arange(CX, dtype=jnp.int32)[None, None, :, None, None, None]
    pencil_y = jnp.arange(CY, dtype=jnp.int32)[None, None, None, :, None, None]
    step_x = jnp.arange(5, dtype=jnp.int32)[None, None, None, None, :, None] - 2
    step_y = jnp.arange(5, dtype=jnp.int32)[None, None, None, None, None, :] - 2
    centre = padded[lane_d * CX + pencil_x + 2, lane_g * CY + pencil_y + 2]
    other = padded[lane_d * CX + pencil_x + 2 + step_x, lane_g * CY + pencil_y + 2 + step_y]
    keep_mask = centre & other
    full_shape = keep_mask.shape
    first_ids = jnp.broadcast_to(pencil_x * CY + pencil_y, full_shape).reshape(N_GY, N_GX, npair)
    second_ids = jnp.broadcast_to((pencil_x + 2 + step_x) * (CY + 4) + pencil_y + 2 + step_y, full_shape).reshape(N_GY, N_GX, npair)
    keep_mask = keep_mask.reshape(N_GY, N_GX, npair)
    perm_keys = jax.random.split(jax.random.fold_in(key, 104), N_GY * N_GX)
    shuffle = jax.vmap(lambda sub_key: jax.random.permutation(sub_key, npair))(perm_keys).astype(jnp.int32)
    score_ids = jnp.where(keep_mask, 0, npair) + shuffle.reshape(N_GY, N_GX, npair)
    sort_order = jnp.argsort(score_ids, axis=2, stable=True)
    keep_sorted = jnp.take_along_axis(keep_mask, sort_order, axis=2)
    first_sorted = jnp.where(keep_sorted, jnp.take_along_axis(first_ids, sort_order, axis=2), 0)
    second_sorted = jnp.where(keep_sorted, jnp.take_along_axis(second_ids, sort_order, axis=2), ext_count)
    stacked = jnp.stack([first_sorted, second_sorted], axis=1)
    return stacked.reshape(N_GY, 2, N_GX * npair).astype(jnp.int32)


def draw_particles(key, part):
    dest_ids, slot_ids, occupied = shared_layout(key)
    pencil_slots = NZ * CAP
    pencil_of = slot_ids // pencil_slots
    inside = slot_ids % pencil_slots
    row_axis = jnp.arange(N_GY, dtype=jnp.int32)[:, None, None]
    base_x = (dest_ids * CX + pencil_of // CY).astype(jnp.float32)
    base_y = (row_axis * CY + pencil_of % CY).astype(jnp.float32)
    base_z = (inside // CAP).astype(jnp.float32)
    draw_shape = dest_ids.shape
    jitter = jax.random.uniform(jax.random.fold_in(key, 201), (3,) + draw_shape, jnp.float32)
    velocity = jnp.clip(jax.random.normal(jax.random.fold_in(key, 202), (3,) + draw_shape, jnp.float32), -4.0, 4.0)
    masses = jnp.exp(jax.random.uniform(jax.random.fold_in(key, 203), draw_shape, jnp.float32, -math.log(2.0), math.log(2.0))) / 8.0
    stacked = jnp.stack([base_x + jitter[0], base_y + jitter[1], base_z + jitter[2], velocity[0], velocity[1], velocity[2], masses], axis=1)
    return stacked.reshape(N_GY, 7, N_GX * PART_DEV).astype(jnp.float32)


def setup_inputs(seed: int = 0) -> dict:
    splits = jax.random.split(jax.random.key(seed), 4)
    return {
        "particles": draw_particles(jax.random.fold_in(splits[3], 71), 0),
        "routing": draw_routing(jax.random.fold_in(splits[3], 71), 0),
        "tile_list": draw_tile_list(jax.random.fold_in(splits[3], 71), 0),
    }


kernel_norm = 21.0 / (16.0 * math.pi)
sound_speed = 2.0
rest_density = 1.0
gravity = 1.0
visc_alpha = 0.5
eta_square = 0.01
pair_block = 64

def kernel_value(dist_sq):
    radius = jnp.sqrt(dist_sq)
    falloff = jnp.maximum(1.0 - 0.5 * radius, 0.0)
    return kernel_norm * falloff ** 4 * (1.0 + 2.0 * radius)

def pressure_term(density):
    pressure = sound_speed * sound_speed * rest_density / 7.0 * ((density / rest_density) ** 7 - 1.0)
    return pressure / (density * density)

def density_blocks(first_ids, second_ids, pair_count, pos_left, grid_right, density_init):

    def advance(block_idx, density):
        start_at = block_idx * pair_block
        left_ids = lax.dynamic_slice_in_dim(first_ids, start_at, pair_block)
        right_ids = lax.dynamic_slice_in_dim(second_ids, start_at, pair_block)
        rows_left = jnp.take(pos_left, left_ids, axis=1)
        rows_right = jnp.take(grid_right, right_ids, axis=1)
        diff_x = rows_left[0][:, :, None] - rows_right[0][:, None, :]
        diff_y = rows_left[1][:, :, None] - rows_right[1][:, None, :]
        diff_z = rows_left[2][:, :, None] - rows_right[2][:, None, :]
        dist_sq = diff_x * diff_x + diff_y * diff_y + diff_z * diff_z
        weight = kernel_value(dist_sq) * rows_right[3][:, None, :]
        return density.at[left_ids].add(lax.optimization_barrier(jnp.sum(weight, axis=2)))
    blocks = ((pair_count + pair_block - 1) // pair_block).astype(jnp.int32)
    return lax.fori_loop(0, blocks, advance, density_init)

def force_blocks(first_ids, second_ids, pair_count, rows_a, rows_b):

    def advance(block_idx, accel):
        start_at = block_idx * pair_block
        left_ids = lax.dynamic_slice_in_dim(first_ids, start_at, pair_block)
        right_ids = lax.dynamic_slice_in_dim(second_ids, start_at, pair_block)
        rows_left = jnp.take(rows_a, left_ids, axis=1)
        rows_right = jnp.take(rows_b, right_ids, axis=1)
        diff_x = rows_left[0][:, :, None] - rows_right[0][:, None, :]
        diff_y = rows_left[1][:, :, None] - rows_right[1][:, None, :]
        diff_z = rows_left[2][:, :, None] - rows_right[2][:, None, :]
        dist_sq = diff_x * diff_x + diff_y * diff_y + diff_z * diff_z
        radius = jnp.sqrt(dist_sq)
        falloff = jnp.maximum(1.0 - 0.5 * radius, 0.0)
        slope_coef = 5.0 * kernel_norm * falloff ** 3
        vel_dot = (rows_left[3][:, :, None] - rows_right[3][:, None, :]) * diff_x + (rows_left[4][:, :, None] - rows_right[4][:, None, :]) * diff_y + (rows_left[5][:, :, None] - rows_right[5][:, None, :]) * diff_z
        approach = jnp.minimum(vel_dot, 0.0) / (dist_sq + eta_square)
        viscous = -visc_alpha * sound_speed * approach / (0.5 * (rows_left[6][:, :, None] + rows_right[7][:, None, :]))
        pair_coef = rows_right[6][:, None, :] * (rows_left[7][:, :, None] + rows_right[8][:, None, :] + viscous) * slope_coef
        pair_sums = jnp.stack([lax.optimization_barrier(jnp.sum(pair_coef * diff_x, axis=2)), lax.optimization_barrier(jnp.sum(pair_coef * diff_y, axis=2)), lax.optimization_barrier(jnp.sum(pair_coef * diff_z, axis=2))])
        return accel.at[:, left_ids].add(pair_sums)
    blocks = ((pair_count + pair_block - 1) // pair_block).astype(jnp.int32)
    pencil_total = rows_a.shape[1]
    accel_init = jnp.zeros((3, pencil_total, rows_a.shape[2]), jnp.float32)
    return lax.fori_loop(0, blocks, advance, accel_init)

def reference(particles, routing, tile_list):
    pencil_slots = NZ * CAP
    pencils = CX * CY
    slots_all = pencils * pencil_slots
    ext_count = (CX + 4) * (CY + 4)
    npair = 25 * pencils
    padded_len = (npair + pair_block - 1) // pair_block * pair_block
    target = routing[:, 0, :] * slots_all + routing[:, 1, :]

    def place(values_in, slot_index):
        return jnp.zeros((7, N_GX * slots_all), jnp.float32).at[:, slot_index].set(values_in)
    layout = jax.vmap(place)(particles, target)
    slot_grid = layout.reshape(N_GY, 7, N_GX, CX, CY, pencil_slots)
    slot_grid = slot_grid.transpose(1, 2, 3, 0, 4, 5).reshape(7, N_GX * CX, N_GY * CY, pencil_slots)
    rim_grid = jnp.pad(slot_grid, ((0, 0), (2, 2), (2, 2), (0, 0)))
    devices = jnp.arange(N_GX * N_GY, dtype=jnp.int32)
    zero_index = jnp.zeros((), jnp.int32)

    def lists_of(device):
        row_id = (device // N_GX).astype(jnp.int32)
        col_id = (device % N_GX).astype(jnp.int32)
        listed = lax.dynamic_slice(tile_list, (row_id, zero_index, col_id * npair), (1, 2, npair))[0]
        first_ids = jnp.concatenate([listed[0], jnp.zeros((padded_len - npair,), jnp.int32)])
        second_ids = jnp.concatenate([listed[1], jnp.full((padded_len - npair,), ext_count, jnp.int32)])
        pair_count = jnp.sum((listed[1] < ext_count).astype(jnp.int32)).astype(jnp.int32)
        return (first_ids, second_ids, pair_count)

    def blocks_of(source, device, width):
        row_id = (device // N_GX).astype(jnp.int32)
        col_id = (device % N_GX).astype(jnp.int32)
        depth = source.shape[0]
        piece = lax.dynamic_slice(source, (zero_index, col_id * CX, row_id * CY, zero_index), (depth, CX + 2 * width, CY + 2 * width, pencil_slots))
        return piece.reshape(depth, -1, pencil_slots)

    def with_dummy(values_in):
        return jnp.concatenate([values_in, jnp.zeros((values_in.shape[0], 1, values_in.shape[2]), jnp.float32)], axis=1)

    def density_of(device):
        first_ids, second_ids, pair_count = lists_of(device)
        own_grid = blocks_of(slot_grid, device, 0)
        near_grid = blocks_of(rim_grid, device, 2)
        grid_right = with_dummy(jnp.concatenate([near_grid[0:3], near_grid[6:7]], axis=0))
        return density_blocks(first_ids, second_ids, pair_count, own_grid[0:3], grid_right, jnp.zeros((pencils, pencil_slots), jnp.float32))
    density_dev = lax.map(density_of, devices)
    density_grid = density_dev.reshape(N_GY, N_GX, CX, CY, pencil_slots).transpose(1, 2, 0, 3, 4)
    density_grid = density_grid.reshape(N_GX * CX, N_GY * CY, pencil_slots)
    rho_safe = jnp.where(slot_grid[6] > 0.0, density_grid, rest_density)
    pterm = pressure_term(rho_safe)
    full_grid = jnp.concatenate([slot_grid, rho_safe[None], pterm[None]], axis=0)
    full_rim = jnp.pad(full_grid, ((0, 0), (2, 2), (2, 2), (0, 0)))

    def force_of(device):
        first_ids, second_ids, pair_count = lists_of(device)
        own_grid = blocks_of(full_grid, device, 0)
        near_grid = with_dummy(blocks_of(full_rim, device, 2))
        rows_a = jnp.concatenate([own_grid[0:6], own_grid[7:9]], axis=0)
        return force_blocks(first_ids, second_ids, pair_count, rows_a, near_grid)
    accel_dev = lax.map(force_of, devices)
    accel_dev = accel_dev.at[:, 2].add(-gravity)
    result_dev = jnp.concatenate([accel_dev, density_dev[:, None]], axis=1)
    result_dev = result_dev.reshape(N_GY, N_GX, 4, slots_all).transpose(0, 2, 1, 3).reshape(N_GY, 4, N_GX * slots_all)
    return jax.vmap(lambda result_row, slot_index: jnp.take(result_row, slot_index, axis=1))(result_dev, target)
```

```python
import math

import jax
import jax.numpy as jnp
from jax import lax
from jax.experimental import pallas as pl
from jax.experimental.pallas import tpu as pltpu
from jax.sharding import PartitionSpec as P

CX = 16
CY = 16
NZ = 16
CAP = 8


kernel_norm = 21.0 / (16.0 * math.pi)
sound_speed = 2.0
rest_density = 1.0
gravity = 1.0
visc_alpha = 0.5
eta_square = 0.01
pair_block = 64


def extended(block, sides, width):
    for axis, dim in sides:
        count = lax.axis_size(axis)
        forward = [(i, i + 1) for i in range(count - 1)]
        backward = [(target, source) for source, target in forward]
        low = lax.ppermute(
            lax.slice_in_dim(block, block.shape[dim] - width, None, axis=dim), axis, forward
        )
        high = lax.ppermute(lax.slice_in_dim(block, 0, width, axis=dim), axis, backward)
        block = jnp.concatenate([low, block, high], axis=dim)
    return block


def kernel_value(dist_sq):
    radius = jnp.sqrt(dist_sq)
    falloff = jnp.maximum(1.0 - 0.5 * radius, 0.0)
    return kernel_norm * falloff**4 * (1.0 + 2.0 * radius)


def pressure_term(density):
    pressure = (
        sound_speed * sound_speed * rest_density / 7.0 * ((density / rest_density) ** 7 - 1.0)
    )
    return pressure / (density * density)


def expand_cells(fields, pencil_count):
    depth = fields.shape[0]
    cells = fields.reshape(depth, pencil_count, NZ, CAP).transpose(1, 0, 3, 2)
    wide = jnp.broadcast_to(cells[..., None], cells.shape + (CAP,))
    wide = wide.reshape(pencil_count, depth, CAP, NZ * CAP)
    dummy = jnp.zeros((1, depth, CAP, NZ * CAP), jnp.float32)
    return jnp.concatenate([wide, dummy], axis=0)


def shifted(rows, step):
    shift = (-CAP * step) % (NZ * CAP)
    if shift == 0:
        return rows
    return pltpu.roll(rows, shift, 1)


def density_kernel(first_ref, second_ref, count_ref, own_ref, near_ref, out_ref):
    out_ref[...] = jnp.zeros(out_ref.shape, jnp.float32)

    def body(p, carry):
        a = first_ref[p]
        b = second_ref[p]
        xi = own_ref[a, 0:1, :]
        yi = own_ref[a, 1:2, :]
        zi = own_ref[a, 2:3, :]
        xj = near_ref[b, 0]
        yj = near_ref[b, 1]
        zj = near_ref[b, 2]
        mj = near_ref[b, 3]
        total = jnp.zeros((CAP, NZ * CAP), jnp.float32)
        for step in range(-2, 3):
            dx = xi - shifted(xj, step)
            dy = yi - shifted(yj, step)
            dz = zi - shifted(zj, step)
            dist_sq = dx * dx + dy * dy + dz * dz
            radius = jnp.sqrt(dist_sq)
            falloff = jnp.maximum(1.0 - 0.5 * radius, 0.0)
            sq = falloff * falloff
            weight = kernel_norm * (sq * sq) * (1.0 + 2.0 * radius)
            total = total + weight * shifted(mj, step)
        out_ref[a] = out_ref[a] + total
        return carry

    lax.fori_loop(0, count_ref[0], body, 0)


def force_kernel(first_ref, second_ref, count_ref, own_ref, near_ref, out_ref):
    out_ref[...] = jnp.zeros(out_ref.shape, jnp.float32)

    def body(p, carry):
        a = first_ref[p]
        b = second_ref[p]
        left = [own_ref[a, k : k + 1, :] for k in range(8)]
        right = [near_ref[b, k] for k in range(9)]
        acc_x = jnp.zeros((CAP, NZ * CAP), jnp.float32)
        acc_y = acc_x
        acc_z = acc_x
        for step in range(-2, 3):
            xj, yj, zj, uj, vj, wj, mj, rj, pj = [shifted(r, step) for r in right]
            dx = left[0] - xj
            dy = left[1] - yj
            dz = left[2] - zj
            dist_sq = dx * dx + dy * dy + dz * dz
            radius = jnp.sqrt(dist_sq)
            falloff = jnp.maximum(1.0 - 0.5 * radius, 0.0)
            slope_coef = 5.0 * kernel_norm * (falloff * falloff * falloff)
            vel_dot = (left[3] - uj) * dx + (left[4] - vj) * dy + (left[5] - wj) * dz
            viscous = (-visc_alpha * sound_speed) * jnp.minimum(vel_dot, 0.0) / (
                (dist_sq + eta_square) * (0.5 * (left[6] + rj))
            )
            pair_coef = mj * (left[7] + pj + viscous) * slope_coef
            acc_x = acc_x + pair_coef * dx
            acc_y = acc_y + pair_coef * dy
            acc_z = acc_z + pair_coef * dz
        out_ref[a, 0] = out_ref[a, 0] + acc_x
        out_ref[a, 1] = out_ref[a, 1] + acc_y
        out_ref[a, 2] = out_ref[a, 2] + acc_z
        return carry

    lax.fori_loop(0, count_ref[0], body, 0)


def pair_pass(kernel, first_ids, second_ids, pair_count, own_rows, near_rows, out_depth):
    pencils = own_rows.shape[0]
    if out_depth == 1:
        out_shape = (pencils, CAP, NZ * CAP)
    else:
        out_shape = (pencils, out_depth, CAP, NZ * CAP)
    vmem = pl.BlockSpec(memory_space=pltpu.VMEM)
    return pl.pallas_call(
        kernel,
        out_shape=jax.ShapeDtypeStruct(out_shape, jnp.float32),
        grid_spec=pltpu.PrefetchScalarGridSpec(
            num_scalar_prefetch=3,
            grid=(1,),
            in_specs=[vmem, vmem],
            out_specs=vmem,
        ),
    )(first_ids, second_ids, pair_count.reshape(1), own_rows, near_rows)


def with_dummy(values_in):
    return jnp.concatenate(
        [values_in, jnp.zeros((values_in.shape[0], 1, values_in.shape[2]), values_in.dtype)], axis=1
    )


def guarded(density, masses):
    return jnp.where(masses > 0.0, density, rest_density)


def local(particles, routing, tile_list):
    lanes_total = lax.axis_size("gx")
    row_count = particles.shape[2]
    capacity = 2 * row_count // lanes_total
    pencil_slots = NZ * CAP
    pencils = CX * CY
    slots_all = pencils * pencil_slots
    ext_count = (CX + 4) * (CY + 4)
    fields = particles[0]
    owner_of = routing[0, 0]
    slot_ids = routing[0, 1]
    owner_ids = jnp.arange(lanes_total, dtype=jnp.int32)
    match_owner = owner_of[None, :] == owner_ids[:, None]
    counts = jnp.sum(match_owner.astype(jnp.int32), axis=1)
    starts = jnp.cumsum(counts) - counts
    within = jnp.arange(capacity, dtype=jnp.int32)
    is_valid = within[None, :] < counts[:, None]
    picked = jnp.where(is_valid, starts[:, None] + within[None, :], 0).reshape(-1)
    packed = jnp.concatenate([fields, slot_ids.astype(jnp.float32)[None, :]], axis=0)
    outgoing = jnp.take(packed, picked, axis=1).reshape(8, lanes_total, capacity)
    marker = jnp.where(is_valid, outgoing[7], float(slots_all))
    outgoing = jnp.concatenate([outgoing[:7], marker[None]], axis=0)
    arrived = lax.all_to_all(outgoing, "gx", split_axis=1, concat_axis=1, tiled=True)
    arrived_slot = arrived[7].reshape(-1).astype(jnp.int32)
    own_grid = (
        jnp.zeros((7, slots_all), jnp.float32)
        .at[:, arrived_slot]
        .set(arrived[:7].reshape(7, -1), mode="drop")
    )
    own_grid = own_grid.reshape(7, CX, CY, pencil_slots)
    own_flat = own_grid.reshape(7, pencils, pencil_slots)
    mass_own = own_flat[6]
    pos_own = own_flat[0:3]
    first_list = tile_list[0, 0]
    second_list = tile_list[0, 1]
    pair_count = jnp.sum((second_list < ext_count).astype(jnp.int32))
    local_fields = jnp.concatenate([own_grid[0:3], own_grid[6:7]], axis=0)
    near_first = extended(local_fields, (("gx", 1), ("gy", 2)), 2)
    own_pos = jnp.concatenate(
        [pos_own, jnp.zeros((5, pencils, pencil_slots), jnp.float32)], axis=0
    ).transpose(1, 0, 2)
    near_rows = expand_cells(near_first.reshape(4, ext_count, pencil_slots), ext_count)
    density_sums = pair_pass(
        density_kernel, first_list, second_list, pair_count, own_pos, near_rows, 1
    )
    density_own = guarded(jnp.sum(density_sums, axis=1), mass_own)
    second_fields = jnp.concatenate(
        [own_grid[3:6], density_own.reshape(1, CX, CY, pencil_slots)], axis=0
    )
    near_second = extended(second_fields, (("gx", 1), ("gy", 2)), 2)
    pos_near = near_first[0:3]
    mass_near = near_first[3]
    vel_near = near_second[0:3]
    density_near = guarded(near_second[3], mass_near)
    pterm_near = pressure_term(density_near)
    rows_b = jnp.concatenate(
        [pos_near, vel_near, mass_near[None], density_near[None], pterm_near[None]], axis=0
    )
    rows_b = expand_cells(rows_b.reshape(9, ext_count, pencil_slots), ext_count)
    rows_a = jnp.concatenate(
        [own_flat[0:6], density_own[None], pressure_term(density_own)[None]], axis=0
    ).transpose(1, 0, 2)
    accel = pair_pass(force_kernel, first_list, second_list, pair_count, rows_a, rows_b, 3)
    accel = jnp.sum(accel, axis=2).transpose(1, 0, 2)
    accel = accel.at[2].add(-gravity)
    results = jnp.concatenate([accel, density_own[None]], axis=0).reshape(4, slots_all)
    reply = jnp.take(results, jnp.minimum(arrived_slot, slots_all - 1), axis=1).reshape(
        4, lanes_total, capacity
    )
    home_rows = lax.all_to_all(reply, "gx", split_axis=1, concat_axis=1, tiled=True)
    start_of = jnp.sum(jnp.where(match_owner, starts[:, None], 0), axis=0)
    row_index = owner_of * capacity + jnp.arange(row_count, dtype=jnp.int32) - start_of
    answer = jnp.take(home_rows.reshape(4, -1), row_index, axis=1)
    return answer[None]


def solution(mesh):
    in_specs = (P("gy", None, "gx"), P("gy", None, "gx"), P("gy", None, "gx"))
    out_specs = P("gy", None, "gx")
    return jax.shard_map(local, mesh=mesh, in_specs=in_specs, out_specs=out_specs, check_vma=False)
```

```python
import math

import jax
import jax.numpy as jnp
from jax import lax
from jax.experimental import pallas as pl
from jax.experimental.pallas import tpu as pltpu
from jax.sharding import PartitionSpec as P

CX = 16
CY = 16
NZ = 16
CAP = 8


kernel_norm = 21.0 / (16.0 * math.pi)
sound_speed = 2.0
rest_density = 1.0
gravity = 1.0
visc_alpha = 0.5
eta_square = 0.01
pair_block = 64
UNROLL = 4


def extended(block, sides, width):
    for axis, dim in sides:
        count = lax.axis_size(axis)
        forward = [(i, i + 1) for i in range(count - 1)]
        backward = [(target, source) for source, target in forward]
        low = lax.ppermute(
            lax.slice_in_dim(block, block.shape[dim] - width, None, axis=dim), axis, forward
        )
        high = lax.ppermute(lax.slice_in_dim(block, 0, width, axis=dim), axis, backward)
        block = jnp.concatenate([low, block, high], axis=dim)
    return block


def kernel_value(dist_sq):
    radius = jnp.sqrt(dist_sq)
    falloff = jnp.maximum(1.0 - 0.5 * radius, 0.0)
    return kernel_norm * falloff**4 * (1.0 + 2.0 * radius)


def pressure_term(density):
    pressure = (
        sound_speed * sound_speed * rest_density / 7.0 * ((density / rest_density) ** 7 - 1.0)
    )
    return pressure / (density * density)


def expand_cells(fields, pencil_count):
    depth = fields.shape[0]
    cells = fields.reshape(depth, pencil_count, NZ, CAP).transpose(1, 0, 3, 2)
    wide = jnp.broadcast_to(cells[..., None], cells.shape + (CAP,))
    return wide.reshape(pencil_count, depth, CAP, NZ * CAP)


def shifted(rows, step):
    shift = (-CAP * step) % (NZ * CAP)
    if shift == 0:
        return rows
    return pltpu.roll(rows, shift, 1)


def pair_loop(first_ref, second_ref, count_ref, last_pencil, contribution, out_ref):
    count = count_ref[0]

    def body(group, carry):
        sums = []
        for lane in range(UNROLL):
            p = group * UNROLL + lane
            a = first_ref[p]
            b = jnp.minimum(second_ref[p], last_pencil)
            live = p < count
            sums.append((a, [jnp.where(live, t, 0.0) for t in contribution(a, b)]))
        for a, parts in sums:
            for k, t in enumerate(parts):
                out_ref[a, k] = out_ref[a, k] + t
        return carry

    lax.fori_loop(0, (count + UNROLL - 1) // UNROLL, body, 0)


def density_kernel(first_ref, second_ref, count_ref, own_ref, near_ref, out_ref):
    out_ref[...] = jnp.zeros(out_ref.shape, jnp.float32)

    def contribution(a, b):
        xi = own_ref[a, 0:1, :]
        yi = own_ref[a, 1:2, :]
        zi = own_ref[a, 2:3, :]
        xj = near_ref[b, 0]
        yj = near_ref[b, 1]
        zj = near_ref[b, 2]
        mj = near_ref[b, 3]
        total = jnp.zeros((CAP, NZ * CAP), jnp.float32)
        for step in range(-2, 3):
            dx = xi - shifted(xj, step)
            dy = yi - shifted(yj, step)
            dz = zi - shifted(zj, step)
            dist_sq = dx * dx + dy * dy + dz * dz
            radius = jnp.sqrt(dist_sq)
            falloff = jnp.maximum(1.0 - 0.5 * radius, 0.0)
            sq = falloff * falloff
            weight = kernel_norm * (sq * sq) * (1.0 + 2.0 * radius)
            total = total + weight * shifted(mj, step)
        return [total]

    pair_loop(first_ref, second_ref, count_ref, near_ref.shape[0] - 1, contribution, out_ref)


def force_kernel(first_ref, second_ref, count_ref, own_ref, near_ref, out_ref):
    out_ref[...] = jnp.zeros(out_ref.shape, jnp.float32)

    def contribution(a, b):
        left = [own_ref[a, k : k + 1, :] for k in range(8)]
        right = [near_ref[b, k] for k in range(9)]
        acc_x = jnp.zeros((CAP, NZ * CAP), jnp.float32)
        acc_y = acc_x
        acc_z = acc_x
        for step in range(-2, 3):
            xj, yj, zj, uj, vj, wj, mj, rj, pj = [shifted(r, step) for r in right]
            dx = left[0] - xj
            dy = left[1] - yj
            dz = left[2] - zj
            dist_sq = dx * dx + dy * dy + dz * dz
            radius = jnp.sqrt(dist_sq)
            falloff = jnp.maximum(1.0 - 0.5 * radius, 0.0)
            slope_coef = 5.0 * kernel_norm * (falloff * falloff * falloff)
            vel_dot = (left[3] - uj) * dx + (left[4] - vj) * dy + (left[5] - wj) * dz
            viscous = (-visc_alpha * sound_speed) * jnp.minimum(vel_dot, 0.0) / (
                (dist_sq + eta_square) * (0.5 * (left[6] + rj))
            )
            pair_coef = mj * (left[7] + pj + viscous) * slope_coef
            acc_x = acc_x + pair_coef * dx
            acc_y = acc_y + pair_coef * dy
            acc_z = acc_z + pair_coef * dz
        return [acc_x, acc_y, acc_z]

    pair_loop(first_ref, second_ref, count_ref, near_ref.shape[0] - 1, contribution, out_ref)


def pair_pass(kernel, first_ids, second_ids, pair_count, own_rows, near_rows, out_depth):
    pencils = own_rows.shape[0]
    out_shape = (pencils, out_depth, CAP, NZ * CAP)
    vmem = pl.BlockSpec(memory_space=pltpu.VMEM)
    return pl.pallas_call(
        kernel,
        out_shape=jax.ShapeDtypeStruct(out_shape, jnp.float32),
        grid_spec=pltpu.PrefetchScalarGridSpec(
            num_scalar_prefetch=3,
            grid=(1,),
            in_specs=[vmem, vmem],
            out_specs=vmem,
        ),
    )(first_ids, second_ids, pair_count.reshape(1), own_rows, near_rows)


def with_dummy(values_in):
    return jnp.concatenate(
        [values_in, jnp.zeros((values_in.shape[0], 1, values_in.shape[2]), values_in.dtype)], axis=1
    )


def guarded(density, masses):
    return jnp.where(masses > 0.0, density, rest_density)


def local(particles, routing, tile_list):
    lanes_total = lax.axis_size("gx")
    row_count = particles.shape[2]
    capacity = 2 * row_count // lanes_total
    pencil_slots = NZ * CAP
    pencils = CX * CY
    slots_all = pencils * pencil_slots
    ext_count = (CX + 4) * (CY + 4)
    fields = particles[0]
    owner_of = routing[0, 0]
    slot_ids = routing[0, 1]
    owner_ids = jnp.arange(lanes_total, dtype=jnp.int32)
    match_owner = owner_of[None, :] == owner_ids[:, None]
    counts = jnp.sum(match_owner.astype(jnp.int32), axis=1)
    starts = jnp.cumsum(counts) - counts
    within = jnp.arange(capacity, dtype=jnp.int32)
    is_valid = within[None, :] < counts[:, None]
    picked = jnp.where(is_valid, starts[:, None] + within[None, :], 0).reshape(-1)
    packed = jnp.concatenate([fields, slot_ids.astype(jnp.float32)[None, :]], axis=0)
    outgoing = jnp.take(packed, picked, axis=1).reshape(8, lanes_total, capacity)
    marker = jnp.where(is_valid, outgoing[7], float(slots_all))
    outgoing = jnp.concatenate([outgoing[:7], marker[None]], axis=0)
    arrived = lax.all_to_all(outgoing, "gx", split_axis=1, concat_axis=1, tiled=True)
    arrived_slot = arrived[7].reshape(-1).astype(jnp.int32)
    own_grid = (
        jnp.zeros((7, slots_all), jnp.float32)
        .at[:, arrived_slot]
        .set(arrived[:7].reshape(7, -1), mode="drop")
    )
    own_grid = own_grid.reshape(7, CX, CY, pencil_slots)
    own_flat = own_grid.reshape(7, pencils, pencil_slots)
    mass_own = own_flat[6]
    pos_own = own_flat[0:3]
    first_list = tile_list[0, 0]
    second_list = tile_list[0, 1]
    pair_count = jnp.sum((second_list < ext_count).astype(jnp.int32))
    local_fields = jnp.concatenate([own_grid[0:3], own_grid[6:7]], axis=0)
    near_first = extended(local_fields, (("gx", 1), ("gy", 2)), 2)
    own_pos = jnp.concatenate(
        [pos_own, jnp.zeros((5, pencils, pencil_slots), jnp.float32)], axis=0
    ).transpose(1, 0, 2)
    near_rows = expand_cells(near_first.reshape(4, ext_count, pencil_slots), ext_count)
    density_sums = pair_pass(
        density_kernel, first_list, second_list, pair_count, own_pos, near_rows, 1
    )
    density_own = guarded(jnp.sum(density_sums[:, 0], axis=1), mass_own)
    second_fields = jnp.concatenate(
        [own_grid[3:6], density_own.reshape(1, CX, CY, pencil_slots)], axis=0
    )
    near_second = extended(second_fields, (("gx", 1), ("gy", 2)), 2)
    pos_near = near_first[0:3]
    mass_near = near_first[3]
    vel_near = near_second[0:3]
    density_near = guarded(near_second[3], mass_near)
    pterm_near = pressure_term(density_near)
    rows_b = jnp.concatenate(
        [pos_near, vel_near, mass_near[None], density_near[None], pterm_near[None]], axis=0
    )
    rows_b = expand_cells(rows_b.reshape(9, ext_count, pencil_slots), ext_count)
    rows_a = jnp.concatenate(
        [own_flat[0:6], density_own[None], pressure_term(density_own)[None]], axis=0
    ).transpose(1, 0, 2)
    accel = pair_pass(force_kernel, first_list, second_list, pair_count, rows_a, rows_b, 3)
    accel = jnp.sum(accel, axis=2).transpose(1, 0, 2)
    accel = accel.at[2].add(-gravity)
    results = jnp.concatenate([accel, density_own[None]], axis=0).reshape(4, slots_all)
    reply = jnp.take(results, jnp.minimum(arrived_slot, slots_all - 1), axis=1).reshape(
        4, lanes_total, capacity
    )
    home_rows = lax.all_to_all(reply, "gx", split_axis=1, concat_axis=1, tiled=True)
    start_of = jnp.sum(jnp.where(match_owner, starts[:, None], 0), axis=0)
    row_index = owner_of * capacity + jnp.arange(row_count, dtype=jnp.int32) - start_of
    answer = jnp.take(home_rows.reshape(4, -1), row_index, axis=1)
    return answer[None]


def solution(mesh):
    in_specs = (P("gy", None, "gx"), P("gy", None, "gx"), P("gy", None, "gx"))
    out_specs = P("gy", None, "gx")
    return jax.shard_map(local, mesh=mesh, in_specs=in_specs, out_specs=out_specs, check_vma=False)
```

```python
import math

import jax
import jax.numpy as jnp
from jax import lax
from jax.experimental import pallas as pl
from jax.experimental.pallas import tpu as pltpu
from jax.sharding import PartitionSpec as P

CX = 16
CY = 16
NZ = 16
CAP = 8


kernel_norm = 21.0 / (16.0 * math.pi)
sound_speed = 2.0
rest_density = 1.0
gravity = 1.0
visc_alpha = 0.5
eta_square = 0.01
pair_block = 64
UNROLL = 4


def extended(block, sides, width):
    for axis, dim in sides:
        count = lax.axis_size(axis)
        forward = [(i, i + 1) for i in range(count - 1)]
        backward = [(target, source) for source, target in forward]
        low = lax.ppermute(
            lax.slice_in_dim(block, block.shape[dim] - width, None, axis=dim), axis, forward
        )
        high = lax.ppermute(lax.slice_in_dim(block, 0, width, axis=dim), axis, backward)
        block = jnp.concatenate([low, block, high], axis=dim)
    return block


def kernel_value(dist_sq):
    radius = jnp.sqrt(dist_sq)
    falloff = jnp.maximum(1.0 - 0.5 * radius, 0.0)
    return kernel_norm * falloff**4 * (1.0 + 2.0 * radius)


def pressure_term(density):
    pressure = (
        sound_speed * sound_speed * rest_density / 7.0 * ((density / rest_density) ** 7 - 1.0)
    )
    return pressure / (density * density)


def expand_cells(fields, pencil_count):
    depth = fields.shape[0]
    cells = fields.reshape(depth, pencil_count, NZ, CAP).transpose(1, 0, 3, 2)
    wide = jnp.broadcast_to(cells[..., None], cells.shape + (CAP,))
    return wide.reshape(pencil_count, depth, CAP, NZ * CAP)


def shifted(rows, step):
    shift = (-CAP * step) % (NZ * CAP)
    if shift == 0:
        return rows
    return pltpu.roll(rows, shift, 1)


def pair_loop(first_ref, second_ref, count_ref, last_pencil, contribution, out_ref):
    count = count_ref[0]

    def body(group, carry):
        sums = []
        for lane in range(UNROLL):
            p = group * UNROLL + lane
            a = first_ref[p]
            b = jnp.minimum(second_ref[p], last_pencil)
            live = p < count
            sums.append((a, [jnp.where(live, t, 0.0) for t in contribution(a, b)]))
        for a, parts in sums:
            for k, t in enumerate(parts):
                out_ref[a, k] = out_ref[a, k] + t
        return carry

    lax.fori_loop(0, (count + UNROLL - 1) // UNROLL, body, 0)


def density_kernel(first_ref, second_ref, count_ref, own_ref, near_ref, out_ref):
    out_ref[...] = jnp.zeros(out_ref.shape, jnp.float32)

    def contribution(a, b):
        xi = own_ref[a, 0:1, :]
        yi = own_ref[a, 1:2, :]
        zi = own_ref[a, 2:3, :]
        xj = near_ref[b, 0]
        yj = near_ref[b, 1]
        zj = near_ref[b, 2]
        mj = near_ref[b, 3]
        total = jnp.zeros((CAP, NZ * CAP), jnp.float32)
        for step in range(-2, 3):
            dx = xi - shifted(xj, step)
            dy = yi - shifted(yj, step)
            dz = zi - shifted(zj, step)
            dist_sq = dx * dx + dy * dy + dz * dz
            radius = jnp.sqrt(dist_sq)
            falloff = jnp.maximum(1.0 - 0.5 * radius, 0.0)
            sq = falloff * falloff
            weight = kernel_norm * (sq * sq) * (1.0 + 2.0 * radius)
            total = total + weight * shifted(mj, step)
        return [total]

    pair_loop(first_ref, second_ref, count_ref, near_ref.shape[0] - 1, contribution, out_ref)


def force_kernel(first_ref, second_ref, count_ref, own_ref, near_ref, out_ref):
    out_ref[...] = jnp.zeros(out_ref.shape, jnp.float32)

    def contribution(a, b):
        left = [own_ref[a, k : k + 1, :] for k in range(8)]
        right = [near_ref[b, k] for k in range(9)]
        acc_x = jnp.zeros((CAP, NZ * CAP), jnp.float32)
        acc_y = acc_x
        acc_z = acc_x
        for step in range(-2, 3):
            xj, yj, zj, uj, vj, wj, mj, rj, pj = [shifted(r, step) for r in right]
            dx = left[0] - xj
            dy = left[1] - yj
            dz = left[2] - zj
            dist_sq = dx * dx + dy * dy + dz * dz
            radius = jnp.sqrt(dist_sq)
            falloff = jnp.maximum(1.0 - 0.5 * radius, 0.0)
            slope_coef = 5.0 * kernel_norm * (falloff * falloff * falloff)
            vel_dot = (left[3] - uj) * dx + (left[4] - vj) * dy + (left[5] - wj) * dz
            viscous = (-visc_alpha * sound_speed) * jnp.minimum(vel_dot, 0.0) / (
                (dist_sq + eta_square) * (0.5 * (left[6] + rj))
            )
            pair_coef = mj * (left[7] + pj + viscous) * slope_coef
            acc_x = acc_x + pair_coef * dx
            acc_y = acc_y + pair_coef * dy
            acc_z = acc_z + pair_coef * dz
        return [acc_x, acc_y, acc_z]

    pair_loop(first_ref, second_ref, count_ref, near_ref.shape[0] - 1, contribution, out_ref)


def pair_pass(kernel, first_ids, second_ids, pair_count, own_rows, near_rows, out_depth):
    pencils = own_rows.shape[0]
    out_shape = (pencils, out_depth, CAP, NZ * CAP)
    vmem = pl.BlockSpec(memory_space=pltpu.VMEM)
    return pl.pallas_call(
        kernel,
        out_shape=jax.ShapeDtypeStruct(out_shape, jnp.float32),
        grid_spec=pltpu.PrefetchScalarGridSpec(
            num_scalar_prefetch=3,
            grid=(1,),
            in_specs=[vmem, vmem],
            out_specs=vmem,
        ),
    )(first_ids, second_ids, pair_count.reshape(1), own_rows, near_rows)


def with_dummy(values_in):
    return jnp.concatenate(
        [values_in, jnp.zeros((values_in.shape[0], 1, values_in.shape[2]), values_in.dtype)], axis=1
    )


def guarded(density, masses):
    return jnp.where(masses > 0.0, density, rest_density)


HIGHEST = lax.Precision.HIGHEST


def window_maps(counts, starts, capacity, row_count):
    lanes_total = counts.shape[0]
    span = (127 + capacity + 127) // 128
    chunk_total = (row_count + 127) // 128 + span
    first_chunk = starts // 128
    offset = starts % 128
    k = jnp.arange(span * 128, dtype=jnp.int32)
    w = jnp.arange(capacity, dtype=jnp.int32)
    shift_map = (
        (k[None, :, None] == offset[:, None, None] + w[None, None, :])
        & (w[None, None, :] < counts[:, None, None])
    ).astype(jnp.float32)
    t = jnp.arange(chunk_total, dtype=jnp.int32)
    chunk_map = (
        t[None, None, :] == first_chunk[:, None, None] + jnp.arange(span, dtype=jnp.int32)[None, :, None]
    ).astype(jnp.float32).reshape(lanes_total * span, chunk_total)
    return shift_map, chunk_map, chunk_total


def local(particles, routing, tile_list):
    lanes_total = lax.axis_size("gx")
    row_count = particles.shape[2]
    capacity = 2 * row_count // lanes_total
    pencil_slots = NZ * CAP
    pencils = CX * CY
    slots_all = pencils * pencil_slots
    ext_count = (CX + 4) * (CY + 4)
    fields = particles[0]
    owner_of = routing[0, 0]
    slot_ids = routing[0, 1]
    owner_ids = jnp.arange(lanes_total, dtype=jnp.int32)
    match_owner = owner_of[None, :] == owner_ids[:, None]
    counts = jnp.sum(match_owner.astype(jnp.int32), axis=1)
    starts = jnp.cumsum(counts) - counts
    within = jnp.arange(capacity, dtype=jnp.int32)
    is_valid = within[None, :] < counts[:, None]
    packed = jnp.concatenate([fields, slot_ids.astype(jnp.float32)[None, :]], axis=0)
    shift_map, chunk_map, chunk_total = window_maps(counts, starts, capacity, row_count)
    chunked = jnp.pad(packed, ((0, 0), (0, chunk_total * 128 - row_count)))
    windows = jnp.einsum(
        "jt,ftl->fjl", chunk_map, chunked.reshape(8, chunk_total, 128), precision=HIGHEST
    ).reshape(8, lanes_total, -1)
    outgoing = jnp.einsum("fok,okw->fow", windows, shift_map, precision=HIGHEST)
    marker = jnp.where(is_valid, outgoing[7], float(slots_all))
    outgoing = jnp.concatenate([outgoing[:7], marker[None]], axis=0)
    arrived = lax.all_to_all(outgoing, "gx", split_axis=1, concat_axis=1, tiled=True)
    arrived_slot = arrived[7].reshape(-1).astype(jnp.int32)
    own_grid = (
        jnp.zeros((7, slots_all), jnp.float32)
        .at[:, arrived_slot]
        .set(arrived[:7].reshape(7, -1), mode="drop")
    )
    own_grid = own_grid.reshape(7, CX, CY, pencil_slots)
    own_flat = own_grid.reshape(7, pencils, pencil_slots)
    mass_own = own_flat[6]
    pos_own = own_flat[0:3]
    first_list = tile_list[0, 0]
    second_list = tile_list[0, 1]
    pair_count = jnp.sum((second_list < ext_count).astype(jnp.int32))
    local_fields = jnp.concatenate([own_grid[0:3], own_grid[6:7]], axis=0)
    near_first = extended(local_fields, (("gx", 1), ("gy", 2)), 2)
    own_pos = jnp.concatenate(
        [pos_own, jnp.zeros((5, pencils, pencil_slots), jnp.float32)], axis=0
    ).transpose(1, 0, 2)
    near_rows = expand_cells(near_first.reshape(4, ext_count, pencil_slots), ext_count)
    density_sums = pair_pass(
        density_kernel, first_list, second_list, pair_count, own_pos, near_rows, 1
    )
    density_own = guarded(jnp.sum(density_sums[:, 0], axis=1), mass_own)
    second_fields = jnp.concatenate(
        [own_grid[3:6], density_own.reshape(1, CX, CY, pencil_slots)], axis=0
    )
    near_second = extended(second_fields, (("gx", 1), ("gy", 2)), 2)
    pos_near = near_first[0:3]
    mass_near = near_first[3]
    vel_near = near_second[0:3]
    density_near = guarded(near_second[3], mass_near)
    pterm_near = pressure_term(density_near)
    rows_b = jnp.concatenate(
        [pos_near, vel_near, mass_near[None], density_near[None], pterm_near[None]], axis=0
    )
    rows_b = expand_cells(rows_b.reshape(9, ext_count, pencil_slots), ext_count)
    rows_a = jnp.concatenate(
        [own_flat[0:6], density_own[None], pressure_term(density_own)[None]], axis=0
    ).transpose(1, 0, 2)
    accel = pair_pass(force_kernel, first_list, second_list, pair_count, rows_a, rows_b, 3)
    accel = jnp.sum(accel, axis=2).transpose(1, 0, 2)
    accel = accel.at[2].add(-gravity)
    results = jnp.concatenate([accel, density_own[None]], axis=0).reshape(4, slots_all)
    reply = jnp.take(results, jnp.minimum(arrived_slot, slots_all - 1), axis=1).reshape(
        4, lanes_total, capacity
    )
    home_rows = lax.all_to_all(reply, "gx", split_axis=1, concat_axis=1, tiled=True)
    spread = jnp.einsum("fow,okw->fok", jnp.where(is_valid[None], home_rows.reshape(4, lanes_total, capacity), 0.0), shift_map, precision=HIGHEST)
    answer = jnp.einsum(
        "jt,fjl->ftl", chunk_map, spread.reshape(4, chunk_map.shape[0], 128), precision=HIGHEST
    ).reshape(4, chunk_total * 128)[:, :row_count]
    return answer[None]


def solution(mesh):
    in_specs = (P("gy", None, "gx"), P("gy", None, "gx"), P("gy", None, "gx"))
    out_specs = P("gy", None, "gx")
    return jax.shard_map(local, mesh=mesh, in_specs=in_specs, out_specs=out_specs, check_vma=False)
```

```python
import math

import jax
import jax.numpy as jnp
from jax import lax
from jax.experimental import pallas as pl
from jax.experimental.pallas import tpu as pltpu
from jax.sharding import PartitionSpec as P

CX = 16
CY = 16
NZ = 16
CAP = 8


kernel_norm = 21.0 / (16.0 * math.pi)
sound_speed = 2.0
rest_density = 1.0
gravity = 1.0
visc_alpha = 0.5
eta_square = 0.01
pair_block = 64


def extended(block, sides, width):
    for axis, dim in sides:
        count = lax.axis_size(axis)
        forward = [(i, i + 1) for i in range(count - 1)]
        backward = [(target, source) for source, target in forward]
        low = lax.ppermute(
            lax.slice_in_dim(block, block.shape[dim] - width, None, axis=dim), axis, forward
        )
        high = lax.ppermute(lax.slice_in_dim(block, 0, width, axis=dim), axis, backward)
        block = jnp.concatenate([low, block, high], axis=dim)
    return block


def kernel_value(dist_sq):
    radius = jnp.sqrt(dist_sq)
    falloff = jnp.maximum(1.0 - 0.5 * radius, 0.0)
    return kernel_norm * falloff**4 * (1.0 + 2.0 * radius)


def pressure_term(density):
    pressure = (
        sound_speed * sound_speed * rest_density / 7.0 * ((density / rest_density) ** 7 - 1.0)
    )
    return pressure / (density * density)


def expand_cells(fields, pencil_count):
    depth = fields.shape[0]
    cells = fields.reshape(depth, pencil_count, NZ, CAP).transpose(1, 0, 3, 2)
    wide = jnp.broadcast_to(cells[..., None], cells.shape + (CAP,))
    return wide.reshape(pencil_count, depth, CAP, NZ * CAP)


def shifted(rows, step):
    shift = (-CAP * step) % (NZ * CAP)
    if shift == 0:
        return rows
    return pltpu.roll(rows, shift, 1)


def pair_loop(first_ref, second_ref, count_ref, last_pencil, contribution, out_ref, unroll):
    count = count_ref[0]

    def body(group, carry):
        sums = []
        for lane in range(unroll):
            p = group * unroll + lane
            a = first_ref[p]
            b = jnp.minimum(second_ref[p], last_pencil)
            live = p < count
            sums.append((a, [jnp.where(live, t, 0.0) for t in contribution(a, b)]))
        for a, parts in sums:
            for k, t in enumerate(parts):
                out_ref[a, k] = out_ref[a, k] + t
        return carry

    lax.fori_loop(0, (count + unroll - 1) // unroll, body, 0)


def density_kernel(first_ref, second_ref, count_ref, own_ref, near_ref, out_ref):
    out_ref[...] = jnp.zeros(out_ref.shape, jnp.float32)

    def contribution(a, b):
        xi = own_ref[a, 0:1, :]
        yi = own_ref[a, 1:2, :]
        zi = own_ref[a, 2:3, :]
        xj = near_ref[b, 0]
        yj = near_ref[b, 1]
        zj = near_ref[b, 2]
        mj = near_ref[b, 3]
        total = jnp.zeros((CAP, NZ * CAP), jnp.float32)
        for step in range(-2, 3):
            dx = xi - shifted(xj, step)
            dy = yi - shifted(yj, step)
            dz = zi - shifted(zj, step)
            dist_sq = dx * dx + dy * dy + dz * dz
            radius = jnp.sqrt(dist_sq)
            falloff = jnp.maximum(1.0 - 0.5 * radius, 0.0)
            sq = falloff * falloff
            weight = kernel_norm * (sq * sq) * (1.0 + 2.0 * radius)
            total = total + weight * shifted(mj, step)
        return [total]

    pair_loop(first_ref, second_ref, count_ref, near_ref.shape[0] - 1, contribution, out_ref, 8)


def force_kernel(first_ref, second_ref, count_ref, own_ref, near_ref, out_ref):
    out_ref[...] = jnp.zeros(out_ref.shape, jnp.float32)

    def contribution(a, b):
        left = [own_ref[a, k : k + 1, :] for k in range(8)]
        right = [near_ref[b, k] for k in range(9)]
        acc_x = jnp.zeros((CAP, NZ * CAP), jnp.float32)
        acc_y = acc_x
        acc_z = acc_x
        for step in range(-2, 3):
            xj, yj, zj, uj, vj, wj, mj, rj, pj = [shifted(r, step) for r in right]
            dx = left[0] - xj
            dy = left[1] - yj
            dz = left[2] - zj
            dist_sq = dx * dx + dy * dy + dz * dz
            radius = jnp.sqrt(dist_sq)
            falloff = jnp.maximum(1.0 - 0.5 * radius, 0.0)
            slope_coef = 5.0 * kernel_norm * (falloff * falloff * falloff)
            vel_dot = (left[3] - uj) * dx + (left[4] - vj) * dy + (left[5] - wj) * dz
            viscous = (-visc_alpha * sound_speed) * jnp.minimum(vel_dot, 0.0) / (
                (dist_sq + eta_square) * (0.5 * (left[6] + rj))
            )
            pair_coef = mj * (left[7] + pj + viscous) * slope_coef
            acc_x = acc_x + pair_coef * dx
            acc_y = acc_y + pair_coef * dy
            acc_z = acc_z + pair_coef * dz
        return [acc_x, acc_y, acc_z]

    pair_loop(first_ref, second_ref, count_ref, near_ref.shape[0] - 1, contribution, out_ref, 4)


def pair_pass(kernel, first_ids, second_ids, pair_count, own_rows, near_rows, out_depth):
    pencils = own_rows.shape[0]
    out_shape = (pencils, out_depth, CAP, NZ * CAP)
    vmem = pl.BlockSpec(memory_space=pltpu.VMEM)
    return pl.pallas_call(
        kernel,
        out_shape=jax.ShapeDtypeStruct(out_shape, jnp.float32),
        grid_spec=pltpu.PrefetchScalarGridSpec(
            num_scalar_prefetch=3,
            grid=(1,),
            in_specs=[vmem, vmem],
            out_specs=vmem,
        ),
    )(first_ids, second_ids, pair_count.reshape(1), own_rows, near_rows)


def with_dummy(values_in):
    return jnp.concatenate(
        [values_in, jnp.zeros((values_in.shape[0], 1, values_in.shape[2]), values_in.dtype)], axis=1
    )


def guarded(density, masses):
    return jnp.where(masses > 0.0, density, rest_density)


HIGHEST = lax.Precision.HIGHEST


def window_maps(counts, starts, capacity, row_count):
    lanes_total = counts.shape[0]
    span = (127 + capacity + 127) // 128
    chunk_total = (row_count + 127) // 128 + span
    first_chunk = starts // 128
    offset = starts % 128
    k = jnp.arange(span * 128, dtype=jnp.int32)
    w = jnp.arange(capacity, dtype=jnp.int32)
    shift_map = (
        (k[None, :, None] == offset[:, None, None] + w[None, None, :])
        & (w[None, None, :] < counts[:, None, None])
    ).astype(jnp.float32)
    t = jnp.arange(chunk_total, dtype=jnp.int32)
    chunk_map = (
        t[None, None, :] == first_chunk[:, None, None] + jnp.arange(span, dtype=jnp.int32)[None, :, None]
    ).astype(jnp.float32).reshape(lanes_total * span, chunk_total)
    return shift_map, chunk_map, chunk_total


def local(particles, routing, tile_list):
    lanes_total = lax.axis_size("gx")
    row_count = particles.shape[2]
    capacity = 2 * row_count // lanes_total
    pencil_slots = NZ * CAP
    pencils = CX * CY
    slots_all = pencils * pencil_slots
    ext_count = (CX + 4) * (CY + 4)
    fields = particles[0]
    owner_of = routing[0, 0]
    slot_ids = routing[0, 1]
    owner_ids = jnp.arange(lanes_total, dtype=jnp.int32)
    match_owner = owner_of[None, :] == owner_ids[:, None]
    counts = jnp.sum(match_owner.astype(jnp.int32), axis=1)
    starts = jnp.cumsum(counts) - counts
    within = jnp.arange(capacity, dtype=jnp.int32)
    is_valid = within[None, :] < counts[:, None]
    packed = jnp.concatenate([fields, slot_ids.astype(jnp.float32)[None, :]], axis=0)
    shift_map, chunk_map, chunk_total = window_maps(counts, starts, capacity, row_count)
    chunked = jnp.pad(packed, ((0, 0), (0, chunk_total * 128 - row_count)))
    windows = jnp.einsum(
        "jt,ftl->fjl", chunk_map, chunked.reshape(8, chunk_total, 128), precision=HIGHEST
    ).reshape(8, lanes_total, -1)
    outgoing = jnp.einsum("fok,okw->fow", windows, shift_map, precision=HIGHEST)
    marker = jnp.where(is_valid, outgoing[7], float(slots_all))
    outgoing = jnp.concatenate([outgoing[:7], marker[None]], axis=0)
    arrived = lax.all_to_all(outgoing, "gx", split_axis=1, concat_axis=1, tiled=True)
    arrived_slot = arrived[7].reshape(-1).astype(jnp.int32)
    own_grid = (
        jnp.zeros((7, slots_all), jnp.float32)
        .at[:, arrived_slot]
        .set(arrived[:7].reshape(7, -1), mode="drop")
    )
    own_grid = own_grid.reshape(7, CX, CY, pencil_slots)
    own_flat = own_grid.reshape(7, pencils, pencil_slots)
    mass_own = own_flat[6]
    pos_own = own_flat[0:3]
    first_list = tile_list[0, 0]
    second_list = tile_list[0, 1]
    pair_count = jnp.sum((second_list < ext_count).astype(jnp.int32))
    local_fields = jnp.concatenate([own_grid[0:3], own_grid[6:7]], axis=0)
    near_first = extended(local_fields, (("gx", 1), ("gy", 2)), 2)
    own_pos = jnp.concatenate(
        [pos_own, jnp.zeros((5, pencils, pencil_slots), jnp.float32)], axis=0
    ).transpose(1, 0, 2)
    near_rows = expand_cells(near_first.reshape(4, ext_count, pencil_slots), ext_count)
    density_sums = pair_pass(
        density_kernel, first_list, second_list, pair_count, own_pos, near_rows, 1
    )
    density_own = guarded(jnp.sum(density_sums[:, 0], axis=1), mass_own)
    second_fields = jnp.concatenate(
        [own_grid[3:6], density_own.reshape(1, CX, CY, pencil_slots)], axis=0
    )
    near_second = extended(second_fields, (("gx", 1), ("gy", 2)), 2)
    pos_near = near_first[0:3]
    mass_near = near_first[3]
    vel_near = near_second[0:3]
    density_near = guarded(near_second[3], mass_near)
    pterm_near = pressure_term(density_near)
    rows_b = jnp.concatenate(
        [pos_near, vel_near, mass_near[None], density_near[None], pterm_near[None]], axis=0
    )
    rows_b = expand_cells(rows_b.reshape(9, ext_count, pencil_slots), ext_count)
    rows_a = jnp.concatenate(
        [own_flat[0:6], density_own[None], pressure_term(density_own)[None]], axis=0
    ).transpose(1, 0, 2)
    accel = pair_pass(force_kernel, first_list, second_list, pair_count, rows_a, rows_b, 3)
    accel = jnp.sum(accel, axis=2).transpose(1, 0, 2)
    accel = accel.at[2].add(-gravity)
    results = jnp.concatenate([accel, density_own[None]], axis=0).reshape(4, slots_all)
    reply = jnp.take(results, jnp.minimum(arrived_slot, slots_all - 1), axis=1).reshape(
        4, lanes_total, capacity
    )
    home_rows = lax.all_to_all(reply, "gx", split_axis=1, concat_axis=1, tiled=True)
    spread = jnp.einsum("fow,okw->fok", jnp.where(is_valid[None], home_rows.reshape(4, lanes_total, capacity), 0.0), shift_map, precision=HIGHEST)
    answer = jnp.einsum(
        "jt,fjl->ftl", chunk_map, spread.reshape(4, chunk_map.shape[0], 128), precision=HIGHEST
    ).reshape(4, chunk_total * 128)[:, :row_count]
    return answer[None]


def solution(mesh):
    in_specs = (P("gy", None, "gx"), P("gy", None, "gx"), P("gy", None, "gx"))
    out_specs = P("gy", None, "gx")
    return jax.shard_map(local, mesh=mesh, in_specs=in_specs, out_specs=out_specs, check_vma=False)
```

```python
import math

import jax
import jax.numpy as jnp
from jax import lax
from jax.experimental import pallas as pl
from jax.experimental.pallas import tpu as pltpu
from jax.sharding import PartitionSpec as P

CX = 16
CY = 16
NZ = 16
CAP = 8


kernel_norm = 21.0 / (16.0 * math.pi)
sound_speed = 2.0
rest_density = 1.0
gravity = 1.0
visc_alpha = 0.5
eta_square = 0.01
pair_block = 64


def extended(block, sides, width):
    for axis, dim in sides:
        count = lax.axis_size(axis)
        forward = [(i, i + 1) for i in range(count - 1)]
        backward = [(target, source) for source, target in forward]
        low = lax.ppermute(
            lax.slice_in_dim(block, block.shape[dim] - width, None, axis=dim), axis, forward
        )
        high = lax.ppermute(lax.slice_in_dim(block, 0, width, axis=dim), axis, backward)
        block = jnp.concatenate([low, block, high], axis=dim)
    return block


def kernel_value(dist_sq):
    radius = jnp.sqrt(dist_sq)
    falloff = jnp.maximum(1.0 - 0.5 * radius, 0.0)
    return kernel_norm * falloff**4 * (1.0 + 2.0 * radius)


def pressure_term(density):
    pressure = (
        sound_speed * sound_speed * rest_density / 7.0 * ((density / rest_density) ** 7 - 1.0)
    )
    return pressure / (density * density)


def expand_cells(fields, pencil_count):
    depth = fields.shape[0]
    cells = fields.reshape(depth, pencil_count, NZ, CAP).transpose(1, 0, 3, 2)
    wide = jnp.broadcast_to(cells[..., None], cells.shape + (CAP,))
    return wide.reshape(pencil_count, depth, CAP, NZ * CAP)


def shifted(rows, step):
    shift = (-CAP * step) % (NZ * CAP)
    if shift == 0:
        return rows
    return pltpu.roll(rows, shift, 1)


def pair_loop(first_ref, second_ref, count_ref, last_pencil, contribution, out_ref, unroll):
    count = count_ref[0]

    def body(group, carry):
        sums = []
        for lane in range(unroll):
            p = group * unroll + lane
            a = first_ref[p]
            b = jnp.minimum(second_ref[p], last_pencil)
            live = p < count
            sums.append((a, [jnp.where(live, t, 0.0) for t in contribution(a, b)]))
        for a, parts in sums:
            for k, t in enumerate(parts):
                out_ref[a, k] = out_ref[a, k] + t
        return carry

    lax.fori_loop(0, (count + unroll - 1) // unroll, body, 0)


def density_kernel(first_ref, second_ref, count_ref, own_ref, near_ref, out_ref):
    out_ref[...] = jnp.zeros(out_ref.shape, jnp.float32)

    def contribution(a, b):
        xi = own_ref[a, 0:1, :]
        yi = own_ref[a, 1:2, :]
        zi = own_ref[a, 2:3, :]
        xj = near_ref[b, 0]
        yj = near_ref[b, 1]
        zj = near_ref[b, 2]
        mj = near_ref[b, 3]
        total = jnp.zeros((CAP, NZ * CAP), jnp.float32)
        for step in range(-2, 3):
            dx = xi - shifted(xj, step)
            dy = yi - shifted(yj, step)
            dz = zi - shifted(zj, step)
            dist_sq = dx * dx + dy * dy + dz * dz
            radius = jnp.sqrt(dist_sq)
            falloff = jnp.maximum(1.0 - 0.5 * radius, 0.0)
            sq = falloff * falloff
            weight = kernel_norm * (sq * sq) * (1.0 + 2.0 * radius)
            total = total + weight * shifted(mj, step)
        return [total]

    pair_loop(first_ref, second_ref, count_ref, near_ref.shape[0] - 1, contribution, out_ref, 8)


def force_kernel(first_ref, second_ref, count_ref, own_ref, near_ref, out_ref):
    out_ref[...] = jnp.zeros(out_ref.shape, jnp.float32)

    def contribution(a, b):
        left = [own_ref[a, k : k + 1, :] for k in range(8)]
        right = [near_ref[b, k] for k in range(9)]
        acc_x = jnp.zeros((CAP, NZ * CAP), jnp.float32)
        acc_y = acc_x
        acc_z = acc_x
        for step in range(-2, 3):
            xj, yj, zj, uj, vj, wj, mj, rj, pj = [shifted(r, step) for r in right]
            dx = left[0] - xj
            dy = left[1] - yj
            dz = left[2] - zj
            dist_sq = dx * dx + dy * dy + dz * dz
            radius = jnp.sqrt(dist_sq)
            falloff = jnp.maximum(1.0 - 0.5 * radius, 0.0)
            slope_coef = 5.0 * kernel_norm * (falloff * falloff * falloff)
            vel_dot = (left[3] - uj) * dx + (left[4] - vj) * dy + (left[5] - wj) * dz
            viscous = (-visc_alpha * sound_speed) * jnp.minimum(vel_dot, 0.0) / (
                (dist_sq + eta_square) * (0.5 * (left[6] + rj))
            )
            pair_coef = mj * (left[7] + pj + viscous) * slope_coef
            acc_x = acc_x + pair_coef * dx
            acc_y = acc_y + pair_coef * dy
            acc_z = acc_z + pair_coef * dz
        return [acc_x, acc_y, acc_z]

    pair_loop(first_ref, second_ref, count_ref, near_ref.shape[0] - 1, contribution, out_ref, 8)


def pair_pass(kernel, first_ids, second_ids, pair_count, own_rows, near_rows, out_depth):
    pencils = own_rows.shape[0]
    out_shape = (pencils, out_depth, CAP, NZ * CAP)
    vmem = pl.BlockSpec(memory_space=pltpu.VMEM)
    return pl.pallas_call(
        kernel,
        out_shape=jax.ShapeDtypeStruct(out_shape, jnp.float32),
        grid_spec=pltpu.PrefetchScalarGridSpec(
            num_scalar_prefetch=3,
            grid=(1,),
            in_specs=[vmem, vmem],
            out_specs=vmem,
        ),
    )(first_ids, second_ids, pair_count.reshape(1), own_rows, near_rows)


def with_dummy(values_in):
    return jnp.concatenate(
        [values_in, jnp.zeros((values_in.shape[0], 1, values_in.shape[2]), values_in.dtype)], axis=1
    )


def guarded(density, masses):
    return jnp.where(masses > 0.0, density, rest_density)


HIGHEST = lax.Precision.HIGHEST


def window_maps(counts, starts, capacity, row_count):
    lanes_total = counts.shape[0]
    span = (127 + capacity + 127) // 128
    chunk_total = (row_count + 127) // 128 + span
    first_chunk = starts // 128
    offset = starts % 128
    k = jnp.arange(span * 128, dtype=jnp.int32)
    w = jnp.arange(capacity, dtype=jnp.int32)
    shift_map = (
        (k[None, :, None] == offset[:, None, None] + w[None, None, :])
        & (w[None, None, :] < counts[:, None, None])
    ).astype(jnp.float32)
    t = jnp.arange(chunk_total, dtype=jnp.int32)
    chunk_map = (
        t[None, None, :] == first_chunk[:, None, None] + jnp.arange(span, dtype=jnp.int32)[None, :, None]
    ).astype(jnp.float32).reshape(lanes_total * span, chunk_total)
    return shift_map, chunk_map, chunk_total


def local(particles, routing, tile_list):
    lanes_total = lax.axis_size("gx")
    row_count = particles.shape[2]
    capacity = 2 * row_count // lanes_total
    pencil_slots = NZ * CAP
    pencils = CX * CY
    slots_all = pencils * pencil_slots
    ext_count = (CX + 4) * (CY + 4)
    fields = particles[0]
    owner_of = routing[0, 0]
    slot_ids = routing[0, 1]
    owner_ids = jnp.arange(lanes_total, dtype=jnp.int32)
    match_owner = owner_of[None, :] == owner_ids[:, None]
    counts = jnp.sum(match_owner.astype(jnp.int32), axis=1)
    starts = jnp.cumsum(counts) - counts
    within = jnp.arange(capacity, dtype=jnp.int32)
    is_valid = within[None, :] < counts[:, None]
    packed = jnp.concatenate([fields, slot_ids.astype(jnp.float32)[None, :]], axis=0)
    shift_map, chunk_map, chunk_total = window_maps(counts, starts, capacity, row_count)
    chunked = jnp.pad(packed, ((0, 0), (0, chunk_total * 128 - row_count)))
    windows = jnp.einsum(
        "jt,ftl->fjl", chunk_map, chunked.reshape(8, chunk_total, 128), precision=HIGHEST
    ).reshape(8, lanes_total, -1)
    outgoing = jnp.einsum("fok,okw->fow", windows, shift_map, precision=HIGHEST)
    marker = jnp.where(is_valid, outgoing[7], float(slots_all))
    outgoing = jnp.concatenate([outgoing[:7], marker[None]], axis=0)
    arrived = lax.all_to_all(outgoing, "gx", split_axis=1, concat_axis=1, tiled=True)
    arrived_slot = arrived[7].reshape(-1).astype(jnp.int32)
    own_grid = (
        jnp.zeros((7, slots_all), jnp.float32)
        .at[:, arrived_slot]
        .set(arrived[:7].reshape(7, -1), mode="drop")
    )
    own_grid = own_grid.reshape(7, CX, CY, pencil_slots)
    own_flat = own_grid.reshape(7, pencils, pencil_slots)
    mass_own = own_flat[6]
    pos_own = own_flat[0:3]
    first_list = tile_list[0, 0]
    second_list = tile_list[0, 1]
    pair_count = jnp.sum((second_list < ext_count).astype(jnp.int32))
    local_fields = jnp.concatenate([own_grid[0:3], own_grid[6:7]], axis=0)
    near_first = extended(local_fields, (("gx", 1), ("gy", 2)), 2)
    own_pos = jnp.concatenate(
        [pos_own, jnp.zeros((5, pencils, pencil_slots), jnp.float32)], axis=0
    ).transpose(1, 0, 2)
    near_rows = expand_cells(near_first.reshape(4, ext_count, pencil_slots), ext_count)
    density_sums = pair_pass(
        density_kernel, first_list, second_list, pair_count, own_pos, near_rows, 1
    )
    density_own = guarded(jnp.sum(density_sums[:, 0], axis=1), mass_own)
    second_fields = jnp.concatenate(
        [own_grid[3:6], density_own.reshape(1, CX, CY, pencil_slots)], axis=0
    )
    near_second = extended(second_fields, (("gx", 1), ("gy", 2)), 2)
    pos_near = near_first[0:3]
    mass_near = near_first[3]
    vel_near = near_second[0:3]
    density_near = guarded(near_second[3], mass_near)
    pterm_near = pressure_term(density_near)
    rows_b = jnp.concatenate(
        [pos_near, vel_near, mass_near[None], density_near[None], pterm_near[None]], axis=0
    )
    rows_b = expand_cells(rows_b.reshape(9, ext_count, pencil_slots), ext_count)
    rows_a = jnp.concatenate(
        [own_flat[0:6], density_own[None], pressure_term(density_own)[None]], axis=0
    ).transpose(1, 0, 2)
    accel = pair_pass(force_kernel, first_list, second_list, pair_count, rows_a, rows_b, 3)
    accel = jnp.sum(accel, axis=2).transpose(1, 0, 2)
    accel = accel.at[2].add(-gravity)
    results = jnp.concatenate([accel, density_own[None]], axis=0).reshape(4, slots_all)
    reply = jnp.take(results, jnp.minimum(arrived_slot, slots_all - 1), axis=1).reshape(
        4, lanes_total, capacity
    )
    home_rows = lax.all_to_all(reply, "gx", split_axis=1, concat_axis=1, tiled=True)
    spread = jnp.einsum("fow,okw->fok", jnp.where(is_valid[None], home_rows.reshape(4, lanes_total, capacity), 0.0), shift_map, precision=HIGHEST)
    answer = jnp.einsum(
        "jt,fjl->ftl", chunk_map, spread.reshape(4, chunk_map.shape[0], 128), precision=HIGHEST
    ).reshape(4, chunk_total * 128)[:, :row_count]
    return answer[None]


def solution(mesh):
    in_specs = (P("gy", None, "gx"), P("gy", None, "gx"), P("gy", None, "gx"))
    out_specs = P("gy", None, "gx")
    return jax.shard_map(local, mesh=mesh, in_specs=in_specs, out_specs=out_specs, check_vma=False)
```

```python
import math

import jax
import jax.numpy as jnp
from jax import lax
from jax.experimental import pallas as pl
from jax.experimental.pallas import tpu as pltpu
from jax.sharding import PartitionSpec as P

CX = 16
CY = 16
NZ = 16
CAP = 8


kernel_norm = 21.0 / (16.0 * math.pi)
sound_speed = 2.0
rest_density = 1.0
gravity = 1.0
visc_alpha = 0.5
eta_square = 0.01
pair_block = 64


def extended(block, sides, width):
    for axis, dim in sides:
        count = lax.axis_size(axis)
        forward = [(i, i + 1) for i in range(count - 1)]
        backward = [(target, source) for source, target in forward]
        low = lax.ppermute(
            lax.slice_in_dim(block, block.shape[dim] - width, None, axis=dim), axis, forward
        )
        high = lax.ppermute(lax.slice_in_dim(block, 0, width, axis=dim), axis, backward)
        block = jnp.concatenate([low, block, high], axis=dim)
    return block


def kernel_value(dist_sq):
    radius = jnp.sqrt(dist_sq)
    falloff = jnp.maximum(1.0 - 0.5 * radius, 0.0)
    return kernel_norm * falloff**4 * (1.0 + 2.0 * radius)


def pressure_term(density):
    pressure = (
        sound_speed * sound_speed * rest_density / 7.0 * ((density / rest_density) ** 7 - 1.0)
    )
    return pressure / (density * density)


def expand_cells(fields, pencil_count):
    depth = fields.shape[0]
    cells = fields.reshape(depth, pencil_count, NZ, CAP).transpose(1, 0, 3, 2)
    wide = jnp.broadcast_to(cells[..., None], cells.shape + (CAP,))
    return wide.reshape(pencil_count, depth, CAP, NZ * CAP)


def shifted(rows, step):
    shift = (-CAP * step) % (NZ * CAP)
    if shift == 0:
        return rows
    return pltpu.roll(rows, shift, 1)


def pair_loop(first_ref, second_ref, count_ref, last_pencil, contribution, out_ref, unroll):
    count = count_ref[0]

    def body(group, carry):
        sums = []
        for lane in range(unroll):
            p = group * unroll + lane
            a = first_ref[p]
            b = jnp.minimum(second_ref[p], last_pencil)
            live = p < count
            sums.append((a, [jnp.where(live, t, 0.0) for t in contribution(a, b)]))
        for a, parts in sums:
            for k, t in enumerate(parts):
                out_ref[a, k] = out_ref[a, k] + t
        return carry

    lax.fori_loop(0, (count + unroll - 1) // unroll, body, 0)


def density_kernel(first_ref, second_ref, count_ref, own_ref, near_ref, out_ref):
    out_ref[...] = jnp.zeros(out_ref.shape, jnp.float32)

    def contribution(a, b):
        xi = own_ref[a, 0:1, :]
        yi = own_ref[a, 1:2, :]
        zi = own_ref[a, 2:3, :]
        xj = near_ref[b, 0]
        yj = near_ref[b, 1]
        zj = near_ref[b, 2]
        mj = near_ref[b, 3]
        total = jnp.zeros((CAP, NZ * CAP), jnp.float32)
        for step in range(-2, 3):
            dx = xi - shifted(xj, step)
            dy = yi - shifted(yj, step)
            dz = zi - shifted(zj, step)
            dist_sq = dx * dx + dy * dy + dz * dz
            radius = jnp.sqrt(dist_sq)
            falloff = jnp.maximum(1.0 - 0.5 * radius, 0.0)
            sq = falloff * falloff
            weight = kernel_norm * (sq * sq) * (1.0 + 2.0 * radius)
            total = total + weight * shifted(mj, step)
        return [total]

    pair_loop(first_ref, second_ref, count_ref, near_ref.shape[0] - 1, contribution, out_ref, 16)


def force_kernel(first_ref, second_ref, count_ref, own_ref, near_ref, out_ref):
    out_ref[...] = jnp.zeros(out_ref.shape, jnp.float32)

    def contribution(a, b):
        left = [own_ref[a, k : k + 1, :] for k in range(8)]
        right = [near_ref[b, k] for k in range(9)]
        acc_x = jnp.zeros((CAP, NZ * CAP), jnp.float32)
        acc_y = acc_x
        acc_z = acc_x
        for step in range(-2, 3):
            xj, yj, zj, uj, vj, wj, mj, rj, pj = [shifted(r, step) for r in right]
            dx = left[0] - xj
            dy = left[1] - yj
            dz = left[2] - zj
            dist_sq = dx * dx + dy * dy + dz * dz
            radius = jnp.sqrt(dist_sq)
            falloff = jnp.maximum(1.0 - 0.5 * radius, 0.0)
            slope_coef = 5.0 * kernel_norm * (falloff * falloff * falloff)
            vel_dot = (left[3] - uj) * dx + (left[4] - vj) * dy + (left[5] - wj) * dz
            viscous = (-visc_alpha * sound_speed) * jnp.minimum(vel_dot, 0.0) / (
                (dist_sq + eta_square) * (0.5 * (left[6] + rj))
            )
            pair_coef = mj * (left[7] + pj + viscous) * slope_coef
            acc_x = acc_x + pair_coef * dx
            acc_y = acc_y + pair_coef * dy
            acc_z = acc_z + pair_coef * dz
        return [acc_x, acc_y, acc_z]

    pair_loop(first_ref, second_ref, count_ref, near_ref.shape[0] - 1, contribution, out_ref, 16)


def pair_pass(kernel, first_ids, second_ids, pair_count, own_rows, near_rows, out_depth):
    pencils = own_rows.shape[0]
    out_shape = (pencils, out_depth, CAP, NZ * CAP)
    vmem = pl.BlockSpec(memory_space=pltpu.VMEM)
    return pl.pallas_call(
        kernel,
        out_shape=jax.ShapeDtypeStruct(out_shape, jnp.float32),
        grid_spec=pltpu.PrefetchScalarGridSpec(
            num_scalar_prefetch=3,
            grid=(1,),
            in_specs=[vmem, vmem],
            out_specs=vmem,
        ),
    )(first_ids, second_ids, pair_count.reshape(1), own_rows, near_rows)


def with_dummy(values_in):
    return jnp.concatenate(
        [values_in, jnp.zeros((values_in.shape[0], 1, values_in.shape[2]), values_in.dtype)], axis=1
    )


def guarded(density, masses):
    return jnp.where(masses > 0.0, density, rest_density)


HIGHEST = lax.Precision.HIGHEST


def window_maps(counts, starts, capacity, row_count):
    lanes_total = counts.shape[0]
    span = (127 + capacity + 127) // 128
    chunk_total = (row_count + 127) // 128 + span
    first_chunk = starts // 128
    offset = starts % 128
    k = jnp.arange(span * 128, dtype=jnp.int32)
    w = jnp.arange(capacity, dtype=jnp.int32)
    shift_map = (
        (k[None, :, None] == offset[:, None, None] + w[None, None, :])
        & (w[None, None, :] < counts[:, None, None])
    ).astype(jnp.float32)
    t = jnp.arange(chunk_total, dtype=jnp.int32)
    chunk_map = (
        t[None, None, :] == first_chunk[:, None, None] + jnp.arange(span, dtype=jnp.int32)[None, :, None]
    ).astype(jnp.float32).reshape(lanes_total * span, chunk_total)
    return shift_map, chunk_map, chunk_total


def local(particles, routing, tile_list):
    lanes_total = lax.axis_size("gx")
    row_count = particles.shape[2]
    capacity = 2 * row_count // lanes_total
    pencil_slots = NZ * CAP
    pencils = CX * CY
    slots_all = pencils * pencil_slots
    ext_count = (CX + 4) * (CY + 4)
    fields = particles[0]
    owner_of = routing[0, 0]
    slot_ids = routing[0, 1]
    owner_ids = jnp.arange(lanes_total, dtype=jnp.int32)
    match_owner = owner_of[None, :] == owner_ids[:, None]
    counts = jnp.sum(match_owner.astype(jnp.int32), axis=1)
    starts = jnp.cumsum(counts) - counts
    within = jnp.arange(capacity, dtype=jnp.int32)
    is_valid = within[None, :] < counts[:, None]
    packed = jnp.concatenate([fields, slot_ids.astype(jnp.float32)[None, :]], axis=0)
    shift_map, chunk_map, chunk_total = window_maps(counts, starts, capacity, row_count)
    chunked = jnp.pad(packed, ((0, 0), (0, chunk_total * 128 - row_count)))
    windows = jnp.einsum(
        "jt,ftl->fjl", chunk_map, chunked.reshape(8, chunk_total, 128), precision=HIGHEST
    ).reshape(8, lanes_total, -1)
    outgoing = jnp.einsum("fok,okw->fow", windows, shift_map, precision=HIGHEST)
    marker = jnp.where(is_valid, outgoing[7], float(slots_all))
    outgoing = jnp.concatenate([outgoing[:7], marker[None]], axis=0)
    arrived = lax.all_to_all(outgoing, "gx", split_axis=1, concat_axis=1, tiled=True)
    arrived_slot = arrived[7].reshape(-1).astype(jnp.int32)
    own_grid = (
        jnp.zeros((7, slots_all), jnp.float32)
        .at[:, arrived_slot]
        .set(arrived[:7].reshape(7, -1), mode="drop")
    )
    own_grid = own_grid.reshape(7, CX, CY, pencil_slots)
    own_flat = own_grid.reshape(7, pencils, pencil_slots)
    mass_own = own_flat[6]
    pos_own = own_flat[0:3]
    first_list = tile_list[0, 0]
    second_list = tile_list[0, 1]
    pair_count = jnp.sum((second_list < ext_count).astype(jnp.int32))
    local_fields = jnp.concatenate([own_grid[0:3], own_grid[6:7]], axis=0)
    near_first = extended(local_fields, (("gx", 1), ("gy", 2)), 2)
    own_pos = jnp.concatenate(
        [pos_own, jnp.zeros((5, pencils, pencil_slots), jnp.float32)], axis=0
    ).transpose(1, 0, 2)
    near_rows = expand_cells(near_first.reshape(4, ext_count, pencil_slots), ext_count)
    density_sums = pair_pass(
        density_kernel, first_list, second_list, pair_count, own_pos, near_rows, 1
    )
    density_own = guarded(jnp.sum(density_sums[:, 0], axis=1), mass_own)
    second_fields = jnp.concatenate(
        [own_grid[3:6], density_own.reshape(1, CX, CY, pencil_slots)], axis=0
    )
    near_second = extended(second_fields, (("gx", 1), ("gy", 2)), 2)
    pos_near = near_first[0:3]
    mass_near = near_first[3]
    vel_near = near_second[0:3]
    density_near = guarded(near_second[3], mass_near)
    pterm_near = pressure_term(density_near)
    rows_b = jnp.concatenate(
        [pos_near, vel_near, mass_near[None], density_near[None], pterm_near[None]], axis=0
    )
    rows_b = expand_cells(rows_b.reshape(9, ext_count, pencil_slots), ext_count)
    rows_a = jnp.concatenate(
        [own_flat[0:6], density_own[None], pressure_term(density_own)[None]], axis=0
    ).transpose(1, 0, 2)
    accel = pair_pass(force_kernel, first_list, second_list, pair_count, rows_a, rows_b, 3)
    accel = jnp.sum(accel, axis=2).transpose(1, 0, 2)
    accel = accel.at[2].add(-gravity)
    results = jnp.concatenate([accel, density_own[None]], axis=0).reshape(4, slots_all)
    reply = jnp.take(results, jnp.minimum(arrived_slot, slots_all - 1), axis=1).reshape(
        4, lanes_total, capacity
    )
    home_rows = lax.all_to_all(reply, "gx", split_axis=1, concat_axis=1, tiled=True)
    spread = jnp.einsum("fow,okw->fok", jnp.where(is_valid[None], home_rows.reshape(4, lanes_total, capacity), 0.0), shift_map, precision=HIGHEST)
    answer = jnp.einsum(
        "jt,fjl->ftl", chunk_map, spread.reshape(4, chunk_map.shape[0], 128), precision=HIGHEST
    ).reshape(4, chunk_total * 128)[:, :row_count]
    return answer[None]


def solution(mesh):
    in_specs = (P("gy", None, "gx"), P("gy", None, "gx"), P("gy", None, "gx"))
    out_specs = P("gy", None, "gx")
    return jax.shard_map(local, mesh=mesh, in_specs=in_specs, out_specs=out_specs, check_vma=False)
```

```python
import math

import jax
import jax.numpy as jnp
from jax import lax
from jax.experimental import pallas as pl
from jax.experimental.pallas import tpu as pltpu
from jax.sharding import PartitionSpec as P

CX = 16
CY = 16
NZ = 16
CAP = 8


kernel_norm = 21.0 / (16.0 * math.pi)
sound_speed = 2.0
rest_density = 1.0
gravity = 1.0
visc_alpha = 0.5
eta_square = 0.01
pair_block = 64


def extended(block, sides, width):
    for axis, dim in sides:
        count = lax.axis_size(axis)
        forward = [(i, i + 1) for i in range(count - 1)]
        backward = [(target, source) for source, target in forward]
        low = lax.ppermute(
            lax.slice_in_dim(block, block.shape[dim] - width, None, axis=dim), axis, forward
        )
        high = lax.ppermute(lax.slice_in_dim(block, 0, width, axis=dim), axis, backward)
        block = jnp.concatenate([low, block, high], axis=dim)
    return block


def kernel_value(dist_sq):
    radius = jnp.sqrt(dist_sq)
    falloff = jnp.maximum(1.0 - 0.5 * radius, 0.0)
    return kernel_norm * falloff**4 * (1.0 + 2.0 * radius)


def pressure_term(density):
    pressure = (
        sound_speed * sound_speed * rest_density / 7.0 * ((density / rest_density) ** 7 - 1.0)
    )
    return pressure / (density * density)


def expand_cells(fields, pencil_count):
    depth = fields.shape[0]
    cells = fields.reshape(depth, pencil_count, NZ, CAP).transpose(1, 0, 3, 2)
    wide = jnp.broadcast_to(cells[..., None], cells.shape + (CAP,))
    return wide.reshape(pencil_count, depth, CAP, NZ * CAP)


def shifted(rows, step):
    shift = (-CAP * step) % (NZ * CAP)
    if shift == 0:
        return rows
    return pltpu.roll(rows, shift, 1)


def pair_loop(first_ref, second_ref, count_ref, last_pencil, contribution, out_ref, unroll):
    count = count_ref[0]

    def body(group, carry):
        sums = []
        for lane in range(unroll):
            p = group * unroll + lane
            a = first_ref[p]
            b = jnp.minimum(second_ref[p], last_pencil)
            live = p < count
            sums.append((a, [jnp.where(live, t, 0.0) for t in contribution(a, b)]))
        for a, parts in sums:
            for k, t in enumerate(parts):
                out_ref[a, k] = out_ref[a, k] + t
        return carry

    lax.fori_loop(0, (count + unroll - 1) // unroll, body, 0)


def density_kernel(first_ref, second_ref, count_ref, own_ref, near_ref, out_ref):
    out_ref[...] = jnp.zeros(out_ref.shape, jnp.float32)

    def contribution(a, b):
        xi = own_ref[a, 0:1, :]
        yi = own_ref[a, 1:2, :]
        zi = own_ref[a, 2:3, :]
        xj = near_ref[b, 0]
        yj = near_ref[b, 1]
        zj = near_ref[b, 2]
        mj = near_ref[b, 3]
        total = jnp.zeros((CAP, NZ * CAP), jnp.float32)
        for step in range(-2, 3):
            dx = xi - shifted(xj, step)
            dy = yi - shifted(yj, step)
            dz = zi - shifted(zj, step)
            dist_sq = dx * dx + dy * dy + dz * dz
            radius = jnp.sqrt(dist_sq)
            falloff = jnp.maximum(1.0 - 0.5 * radius, 0.0)
            sq = falloff * falloff
            weight = kernel_norm * (sq * sq) * (1.0 + 2.0 * radius)
            total = total + weight * shifted(mj, step)
        return [total]

    pair_loop(first_ref, second_ref, count_ref, near_ref.shape[0] - 1, contribution, out_ref, 32)


def force_kernel(first_ref, second_ref, count_ref, own_ref, near_ref, out_ref):
    out_ref[...] = jnp.zeros(out_ref.shape, jnp.float32)

    def contribution(a, b):
        left = [own_ref[a, k : k + 1, :] for k in range(8)]
        right = [near_ref[b, k] for k in range(9)]
        acc_x = jnp.zeros((CAP, NZ * CAP), jnp.float32)
        acc_y = acc_x
        acc_z = acc_x
        for step in range(-2, 3):
            xj, yj, zj, uj, vj, wj, mj, rj, pj = [shifted(r, step) for r in right]
            dx = left[0] - xj
            dy = left[1] - yj
            dz = left[2] - zj
            dist_sq = dx * dx + dy * dy + dz * dz
            radius = jnp.sqrt(dist_sq)
            falloff = jnp.maximum(1.0 - 0.5 * radius, 0.0)
            slope_coef = 5.0 * kernel_norm * (falloff * falloff * falloff)
            vel_dot = (left[3] - uj) * dx + (left[4] - vj) * dy + (left[5] - wj) * dz
            viscous = (-visc_alpha * sound_speed) * jnp.minimum(vel_dot, 0.0) / (
                (dist_sq + eta_square) * (0.5 * (left[6] + rj))
            )
            pair_coef = mj * (left[7] + pj + viscous) * slope_coef
            acc_x = acc_x + pair_coef * dx
            acc_y = acc_y + pair_coef * dy
            acc_z = acc_z + pair_coef * dz
        return [acc_x, acc_y, acc_z]

    pair_loop(first_ref, second_ref, count_ref, near_ref.shape[0] - 1, contribution, out_ref, 32)


def pair_pass(kernel, first_ids, second_ids, pair_count, own_rows, near_rows, out_depth):
    pencils = own_rows.shape[0]
    out_shape = (pencils, out_depth, CAP, NZ * CAP)
    vmem = pl.BlockSpec(memory_space=pltpu.VMEM)
    return pl.pallas_call(
        kernel,
        out_shape=jax.ShapeDtypeStruct(out_shape, jnp.float32),
        grid_spec=pltpu.PrefetchScalarGridSpec(
            num_scalar_prefetch=3,
            grid=(1,),
            in_specs=[vmem, vmem],
            out_specs=vmem,
        ),
    )(first_ids, second_ids, pair_count.reshape(1), own_rows, near_rows)


def with_dummy(values_in):
    return jnp.concatenate(
        [values_in, jnp.zeros((values_in.shape[0], 1, values_in.shape[2]), values_in.dtype)], axis=1
    )


def guarded(density, masses):
    return jnp.where(masses > 0.0, density, rest_density)


HIGHEST = lax.Precision.HIGHEST


def window_maps(counts, starts, capacity, row_count):
    lanes_total = counts.shape[0]
    span = (127 + capacity + 127) // 128
    chunk_total = (row_count + 127) // 128 + span
    first_chunk = starts // 128
    offset = starts % 128
    k = jnp.arange(span * 128, dtype=jnp.int32)
    w = jnp.arange(capacity, dtype=jnp.int32)
    shift_map = (
        (k[None, :, None] == offset[:, None, None] + w[None, None, :])
        & (w[None, None, :] < counts[:, None, None])
    ).astype(jnp.float32)
    t = jnp.arange(chunk_total, dtype=jnp.int32)
    chunk_map = (
        t[None, None, :] == first_chunk[:, None, None] + jnp.arange(span, dtype=jnp.int32)[None, :, None]
    ).astype(jnp.float32).reshape(lanes_total * span, chunk_total)
    return shift_map, chunk_map, chunk_total


def local(particles, routing, tile_list):
    lanes_total = lax.axis_size("gx")
    row_count = particles.shape[2]
    capacity = 2 * row_count // lanes_total
    pencil_slots = NZ * CAP
    pencils = CX * CY
    slots_all = pencils * pencil_slots
    ext_count = (CX + 4) * (CY + 4)
    fields = particles[0]
    owner_of = routing[0, 0]
    slot_ids = routing[0, 1]
    owner_ids = jnp.arange(lanes_total, dtype=jnp.int32)
    match_owner = owner_of[None, :] == owner_ids[:, None]
    counts = jnp.sum(match_owner.astype(jnp.int32), axis=1)
    starts = jnp.cumsum(counts) - counts
    within = jnp.arange(capacity, dtype=jnp.int32)
    is_valid = within[None, :] < counts[:, None]
    packed = jnp.concatenate([fields, slot_ids.astype(jnp.float32)[None, :]], axis=0)
    shift_map, chunk_map, chunk_total = window_maps(counts, starts, capacity, row_count)
    chunked = jnp.pad(packed, ((0, 0), (0, chunk_total * 128 - row_count)))
    windows = jnp.einsum(
        "jt,ftl->fjl", chunk_map, chunked.reshape(8, chunk_total, 128), precision=HIGHEST
    ).reshape(8, lanes_total, -1)
    outgoing = jnp.einsum("fok,okw->fow", windows, shift_map, precision=HIGHEST)
    marker = jnp.where(is_valid, outgoing[7], float(slots_all))
    outgoing = jnp.concatenate([outgoing[:7], marker[None]], axis=0)
    arrived = lax.all_to_all(outgoing, "gx", split_axis=1, concat_axis=1, tiled=True)
    arrived_slot = arrived[7].reshape(-1).astype(jnp.int32)
    own_grid = (
        jnp.zeros((7, slots_all), jnp.float32)
        .at[:, arrived_slot]
        .set(arrived[:7].reshape(7, -1), mode="drop")
    )
    own_grid = own_grid.reshape(7, CX, CY, pencil_slots)
    own_flat = own_grid.reshape(7, pencils, pencil_slots)
    mass_own = own_flat[6]
    pos_own = own_flat[0:3]
    first_list = tile_list[0, 0]
    second_list = tile_list[0, 1]
    pair_count = jnp.sum((second_list < ext_count).astype(jnp.int32))
    local_fields = jnp.concatenate([own_grid[0:3], own_grid[6:7]], axis=0)
    near_first = extended(local_fields, (("gx", 1), ("gy", 2)), 2)
    own_pos = jnp.concatenate(
        [pos_own, jnp.zeros((5, pencils, pencil_slots), jnp.float32)], axis=0
    ).transpose(1, 0, 2)
    near_rows = expand_cells(near_first.reshape(4, ext_count, pencil_slots), ext_count)
    density_sums = pair_pass(
        density_kernel, first_list, second_list, pair_count, own_pos, near_rows, 1
    )
    density_own = guarded(jnp.sum(density_sums[:, 0], axis=1), mass_own)
    second_fields = jnp.concatenate(
        [own_grid[3:6], density_own.reshape(1, CX, CY, pencil_slots)], axis=0
    )
    near_second = extended(second_fields, (("gx", 1), ("gy", 2)), 2)
    pos_near = near_first[0:3]
    mass_near = near_first[3]
    vel_near = near_second[0:3]
    density_near = guarded(near_second[3], mass_near)
    pterm_near = pressure_term(density_near)
    rows_b = jnp.concatenate(
        [pos_near, vel_near, mass_near[None], density_near[None], pterm_near[None]], axis=0
    )
    rows_b = expand_cells(rows_b.reshape(9, ext_count, pencil_slots), ext_count)
    rows_a = jnp.concatenate(
        [own_flat[0:6], density_own[None], pressure_term(density_own)[None]], axis=0
    ).transpose(1, 0, 2)
    accel = pair_pass(force_kernel, first_list, second_list, pair_count, rows_a, rows_b, 3)
    accel = jnp.sum(accel, axis=2).transpose(1, 0, 2)
    accel = accel.at[2].add(-gravity)
    results = jnp.concatenate([accel, density_own[None]], axis=0).reshape(4, slots_all)
    reply = jnp.take(results, jnp.minimum(arrived_slot, slots_all - 1), axis=1).reshape(
        4, lanes_total, capacity
    )
    home_rows = lax.all_to_all(reply, "gx", split_axis=1, concat_axis=1, tiled=True)
    spread = jnp.einsum("fow,okw->fok", jnp.where(is_valid[None], home_rows.reshape(4, lanes_total, capacity), 0.0), shift_map, precision=HIGHEST)
    answer = jnp.einsum(
        "jt,fjl->ftl", chunk_map, spread.reshape(4, chunk_map.shape[0], 128), precision=HIGHEST
    ).reshape(4, chunk_total * 128)[:, :row_count]
    return answer[None]


def solution(mesh):
    in_specs = (P("gy", None, "gx"), P("gy", None, "gx"), P("gy", None, "gx"))
    out_specs = P("gy", None, "gx")
    return jax.shard_map(local, mesh=mesh, in_specs=in_specs, out_specs=out_specs, check_vma=False)
```

```python
import math

import jax
import jax.numpy as jnp
from jax import lax
from jax.experimental import pallas as pl
from jax.experimental.pallas import tpu as pltpu
from jax.sharding import PartitionSpec as P

CX = 16
CY = 16
NZ = 16
CAP = 8


kernel_norm = 21.0 / (16.0 * math.pi)
sound_speed = 2.0
rest_density = 1.0
gravity = 1.0
visc_alpha = 0.5
eta_square = 0.01
pair_block = 64


def extended(block, sides, width):
    for axis, dim in sides:
        count = lax.axis_size(axis)
        forward = [(i, i + 1) for i in range(count - 1)]
        backward = [(target, source) for source, target in forward]
        low = lax.ppermute(
            lax.slice_in_dim(block, block.shape[dim] - width, None, axis=dim), axis, forward
        )
        high = lax.ppermute(lax.slice_in_dim(block, 0, width, axis=dim), axis, backward)
        block = jnp.concatenate([low, block, high], axis=dim)
    return block


def kernel_value(dist_sq):
    radius = jnp.sqrt(dist_sq)
    falloff = jnp.maximum(1.0 - 0.5 * radius, 0.0)
    return kernel_norm * falloff**4 * (1.0 + 2.0 * radius)


def pressure_term(density):
    pressure = (
        sound_speed * sound_speed * rest_density / 7.0 * ((density / rest_density) ** 7 - 1.0)
    )
    return pressure / (density * density)


def expand_cells(fields, pencil_count):
    depth = fields.shape[0]
    cells = fields.reshape(depth, pencil_count, NZ, CAP).transpose(1, 0, 3, 2)
    wide = jnp.broadcast_to(cells[..., None], cells.shape + (CAP,))
    return wide.reshape(pencil_count, depth, CAP, NZ * CAP)


def shifted(rows, step):
    shift = (-CAP * step) % (NZ * CAP)
    if shift == 0:
        return rows
    return pltpu.roll(rows, shift, 1)


def pair_loop(first_ref, second_ref, count_ref, last_pencil, contribution, out_ref, unroll):
    count = count_ref[0]

    def body(group, carry):
        sums = []
        for lane in range(unroll):
            p = group * unroll + lane
            a = first_ref[p]
            b = jnp.minimum(second_ref[p], last_pencil)
            live = p < count
            sums.append((a, [jnp.where(live, t, 0.0) for t in contribution(a, b)]))
        for a, parts in sums:
            for k, t in enumerate(parts):
                out_ref[a, k] = out_ref[a, k] + t
        return carry

    lax.fori_loop(0, (count + unroll - 1) // unroll, body, 0)


def density_kernel(first_ref, second_ref, count_ref, own_ref, near_ref, out_ref):
    out_ref[...] = jnp.zeros(out_ref.shape, jnp.float32)

    def contribution(a, b):
        xi = own_ref[a, 0:1, :]
        yi = own_ref[a, 1:2, :]
        zi = own_ref[a, 2:3, :]
        xj = near_ref[b, 0]
        yj = near_ref[b, 1]
        zj = near_ref[b, 2]
        mj = near_ref[b, 3]
        total = jnp.zeros((CAP, NZ * CAP), jnp.float32)
        for step in range(-2, 3):
            dx = xi - shifted(xj, step)
            dy = yi - shifted(yj, step)
            dz = zi - shifted(zj, step)
            dist_sq = dx * dx + dy * dy + dz * dz
            radius = jnp.sqrt(dist_sq)
            falloff = jnp.maximum(1.0 - 0.5 * radius, 0.0)
            sq = falloff * falloff
            weight = kernel_norm * (sq * sq) * (1.0 + 2.0 * radius)
            total = total + weight * shifted(mj, step)
        return [total]

    pair_loop(first_ref, second_ref, count_ref, near_ref.shape[0] - 1, contribution, out_ref, 64)


def force_kernel(first_ref, second_ref, count_ref, own_ref, near_ref, out_ref):
    out_ref[...] = jnp.zeros(out_ref.shape, jnp.float32)

    def contribution(a, b):
        left = [own_ref[a, k : k + 1, :] for k in range(8)]
        right = [near_ref[b, k] for k in range(9)]
        acc_x = jnp.zeros((CAP, NZ * CAP), jnp.float32)
        acc_y = acc_x
        acc_z = acc_x
        for step in range(-2, 3):
            xj, yj, zj, uj, vj, wj, mj, rj, pj = [shifted(r, step) for r in right]
            dx = left[0] - xj
            dy = left[1] - yj
            dz = left[2] - zj
            dist_sq = dx * dx + dy * dy + dz * dz
            radius = jnp.sqrt(dist_sq)
            falloff = jnp.maximum(1.0 - 0.5 * radius, 0.0)
            slope_coef = 5.0 * kernel_norm * (falloff * falloff * falloff)
            vel_dot = (left[3] - uj) * dx + (left[4] - vj) * dy + (left[5] - wj) * dz
            viscous = (-visc_alpha * sound_speed) * jnp.minimum(vel_dot, 0.0) / (
                (dist_sq + eta_square) * (0.5 * (left[6] + rj))
            )
            pair_coef = mj * (left[7] + pj + viscous) * slope_coef
            acc_x = acc_x + pair_coef * dx
            acc_y = acc_y + pair_coef * dy
            acc_z = acc_z + pair_coef * dz
        return [acc_x, acc_y, acc_z]

    pair_loop(first_ref, second_ref, count_ref, near_ref.shape[0] - 1, contribution, out_ref, 64)


def pair_pass(kernel, first_ids, second_ids, pair_count, own_rows, near_rows, out_depth):
    pencils = own_rows.shape[0]
    out_shape = (pencils, out_depth, CAP, NZ * CAP)
    vmem = pl.BlockSpec(memory_space=pltpu.VMEM)
    return pl.pallas_call(
        kernel,
        out_shape=jax.ShapeDtypeStruct(out_shape, jnp.float32),
        grid_spec=pltpu.PrefetchScalarGridSpec(
            num_scalar_prefetch=3,
            grid=(1,),
            in_specs=[vmem, vmem],
            out_specs=vmem,
        ),
    )(first_ids, second_ids, pair_count.reshape(1), own_rows, near_rows)


def with_dummy(values_in):
    return jnp.concatenate(
        [values_in, jnp.zeros((values_in.shape[0], 1, values_in.shape[2]), values_in.dtype)], axis=1
    )


def guarded(density, masses):
    return jnp.where(masses > 0.0, density, rest_density)


HIGHEST = lax.Precision.HIGHEST


def window_maps(counts, starts, capacity, row_count):
    lanes_total = counts.shape[0]
    span = (127 + capacity + 127) // 128
    chunk_total = (row_count + 127) // 128 + span
    first_chunk = starts // 128
    offset = starts % 128
    k = jnp.arange(span * 128, dtype=jnp.int32)
    w = jnp.arange(capacity, dtype=jnp.int32)
    shift_map = (
        (k[None, :, None] == offset[:, None, None] + w[None, None, :])
        & (w[None, None, :] < counts[:, None, None])
    ).astype(jnp.float32)
    t = jnp.arange(chunk_total, dtype=jnp.int32)
    chunk_map = (
        t[None, None, :] == first_chunk[:, None, None] + jnp.arange(span, dtype=jnp.int32)[None, :, None]
    ).astype(jnp.float32).reshape(lanes_total * span, chunk_total)
    return shift_map, chunk_map, chunk_total


def local(particles, routing, tile_list):
    lanes_total = lax.axis_size("gx")
    row_count = particles.shape[2]
    capacity = 2 * row_count // lanes_total
    pencil_slots = NZ * CAP
    pencils = CX * CY
    slots_all = pencils * pencil_slots
    ext_count = (CX + 4) * (CY + 4)
    fields = particles[0]
    owner_of = routing[0, 0]
    slot_ids = routing[0, 1]
    owner_ids = jnp.arange(lanes_total, dtype=jnp.int32)
    match_owner = owner_of[None, :] == owner_ids[:, None]
    counts = jnp.sum(match_owner.astype(jnp.int32), axis=1)
    starts = jnp.cumsum(counts) - counts
    within = jnp.arange(capacity, dtype=jnp.int32)
    is_valid = within[None, :] < counts[:, None]
    packed = jnp.concatenate([fields, slot_ids.astype(jnp.float32)[None, :]], axis=0)
    shift_map, chunk_map, chunk_total = window_maps(counts, starts, capacity, row_count)
    chunked = jnp.pad(packed, ((0, 0), (0, chunk_total * 128 - row_count)))
    windows = jnp.einsum(
        "jt,ftl->fjl", chunk_map, chunked.reshape(8, chunk_total, 128), precision=HIGHEST
    ).reshape(8, lanes_total, -1)
    outgoing = jnp.einsum("fok,okw->fow", windows, shift_map, precision=HIGHEST)
    marker = jnp.where(is_valid, outgoing[7], float(slots_all))
    outgoing = jnp.concatenate([outgoing[:7], marker[None]], axis=0)
    arrived = lax.all_to_all(outgoing, "gx", split_axis=1, concat_axis=1, tiled=True)
    arrived_slot = arrived[7].reshape(-1).astype(jnp.int32)
    own_grid = (
        jnp.zeros((7, slots_all), jnp.float32)
        .at[:, arrived_slot]
        .set(arrived[:7].reshape(7, -1), mode="drop")
    )
    own_grid = own_grid.reshape(7, CX, CY, pencil_slots)
    own_flat = own_grid.reshape(7, pencils, pencil_slots)
    mass_own = own_flat[6]
    pos_own = own_flat[0:3]
    first_list = tile_list[0, 0]
    second_list = tile_list[0, 1]
    pair_count = jnp.sum((second_list < ext_count).astype(jnp.int32))
    local_fields = jnp.concatenate([own_grid[0:3], own_grid[6:7]], axis=0)
    near_first = extended(local_fields, (("gx", 1), ("gy", 2)), 2)
    own_pos = jnp.concatenate(
        [pos_own, jnp.zeros((5, pencils, pencil_slots), jnp.float32)], axis=0
    ).transpose(1, 0, 2)
    near_rows = expand_cells(near_first.reshape(4, ext_count, pencil_slots), ext_count)
    density_sums = pair_pass(
        density_kernel, first_list, second_list, pair_count, own_pos, near_rows, 1
    )
    density_own = guarded(jnp.sum(density_sums[:, 0], axis=1), mass_own)
    second_fields = jnp.concatenate(
        [own_grid[3:6], density_own.reshape(1, CX, CY, pencil_slots)], axis=0
    )
    near_second = extended(second_fields, (("gx", 1), ("gy", 2)), 2)
    pos_near = near_first[0:3]
    mass_near = near_first[3]
    vel_near = near_second[0:3]
    density_near = guarded(near_second[3], mass_near)
    pterm_near = pressure_term(density_near)
    rows_b = jnp.concatenate(
        [pos_near, vel_near, mass_near[None], density_near[None], pterm_near[None]], axis=0
    )
    rows_b = expand_cells(rows_b.reshape(9, ext_count, pencil_slots), ext_count)
    rows_a = jnp.concatenate(
        [own_flat[0:6], density_own[None], pressure_term(density_own)[None]], axis=0
    ).transpose(1, 0, 2)
    accel = pair_pass(force_kernel, first_list, second_list, pair_count, rows_a, rows_b, 3)
    accel = jnp.sum(accel, axis=2).transpose(1, 0, 2)
    accel = accel.at[2].add(-gravity)
    results = jnp.concatenate([accel, density_own[None]], axis=0).reshape(4, slots_all)
    reply = jnp.take(results, jnp.minimum(arrived_slot, slots_all - 1), axis=1).reshape(
        4, lanes_total, capacity
    )
    home_rows = lax.all_to_all(reply, "gx", split_axis=1, concat_axis=1, tiled=True)
    spread = jnp.einsum("fow,okw->fok", jnp.where(is_valid[None], home_rows.reshape(4, lanes_total, capacity), 0.0), shift_map, precision=HIGHEST)
    answer = jnp.einsum(
        "jt,fjl->ftl", chunk_map, spread.reshape(4, chunk_map.shape[0], 128), precision=HIGHEST
    ).reshape(4, chunk_total * 128)[:, :row_count]
    return answer[None]


def solution(mesh):
    in_specs = (P("gy", None, "gx"), P("gy", None, "gx"), P("gy", None, "gx"))
    out_specs = P("gy", None, "gx")
    return jax.shard_map(local, mesh=mesh, in_specs=in_specs, out_specs=out_specs, check_vma=False)
```

```python
import math

import jax
import jax.numpy as jnp
from jax import lax
from jax.experimental import pallas as pl
from jax.experimental.pallas import tpu as pltpu
from jax.sharding import PartitionSpec as P

CX = 16
CY = 16
NZ = 16
CAP = 8


kernel_norm = 21.0 / (16.0 * math.pi)
sound_speed = 2.0
rest_density = 1.0
gravity = 1.0
visc_alpha = 0.5
eta_square = 0.01
pair_block = 64


def extended(block, sides, width):
    for axis, dim in sides:
        count = lax.axis_size(axis)
        forward = [(i, i + 1) for i in range(count - 1)]
        backward = [(target, source) for source, target in forward]
        low = lax.ppermute(
            lax.slice_in_dim(block, block.shape[dim] - width, None, axis=dim), axis, forward
        )
        high = lax.ppermute(lax.slice_in_dim(block, 0, width, axis=dim), axis, backward)
        block = jnp.concatenate([low, block, high], axis=dim)
    return block


def kernel_value(dist_sq):
    radius = jnp.sqrt(dist_sq)
    falloff = jnp.maximum(1.0 - 0.5 * radius, 0.0)
    return kernel_norm * falloff**4 * (1.0 + 2.0 * radius)


def pressure_term(density):
    pressure = (
        sound_speed * sound_speed * rest_density / 7.0 * ((density / rest_density) ** 7 - 1.0)
    )
    return pressure / (density * density)


def expand_cells(fields, pencil_count):
    depth = fields.shape[0]
    cells = fields.reshape(depth, pencil_count, NZ, CAP).transpose(1, 0, 3, 2)
    wide = jnp.broadcast_to(cells[..., None], cells.shape + (CAP,))
    return wide.reshape(pencil_count, depth, CAP, NZ * CAP)


def shifted(rows, step):
    shift = (-CAP * step) % (NZ * CAP)
    if shift == 0:
        return rows
    return pltpu.roll(rows, shift, 1)


def pair_loop(first_ref, second_ref, count_ref, last_pencil, contribution, out_ref, unroll):
    count = count_ref[0]

    def body(group, carry):
        sums = []
        for lane in range(unroll):
            p = group * unroll + lane
            a = first_ref[p]
            b = jnp.minimum(second_ref[p], last_pencil)
            live = p < count
            sums.append((a, [jnp.where(live, t, 0.0) for t in contribution(a, b)]))
        for a, parts in sums:
            for k, t in enumerate(parts):
                out_ref[a, k] = out_ref[a, k] + t
        return carry

    lax.fori_loop(0, (count + unroll - 1) // unroll, body, 0)


def density_kernel(first_ref, second_ref, count_ref, own_ref, near_ref, out_ref):
    out_ref[...] = jnp.zeros(out_ref.shape, jnp.float32)

    def contribution(a, b):
        xi = own_ref[a, 0:1, :]
        yi = own_ref[a, 1:2, :]
        zi = own_ref[a, 2:3, :]
        xj = near_ref[b, 0]
        yj = near_ref[b, 1]
        zj = near_ref[b, 2]
        mj = near_ref[b, 3]
        total = jnp.zeros((CAP, NZ * CAP), jnp.float32)
        for step in range(-2, 3):
            dx = xi - shifted(xj, step)
            dy = yi - shifted(yj, step)
            dz = zi - shifted(zj, step)
            dist_sq = dx * dx + dy * dy + dz * dz
            radius = jnp.sqrt(dist_sq)
            falloff = jnp.maximum(1.0 - 0.5 * radius, 0.0)
            sq = falloff * falloff
            weight = kernel_norm * (sq * sq) * (1.0 + 2.0 * radius)
            total = total + weight * shifted(mj, step)
        return [total]

    pair_loop(first_ref, second_ref, count_ref, near_ref.shape[0] - 1, contribution, out_ref, 64)


def force_kernel(first_ref, second_ref, count_ref, own_ref, near_ref, out_ref):
    out_ref[...] = jnp.zeros(out_ref.shape, jnp.float32)

    def contribution(a, b):
        left = [own_ref[a, k : k + 1, :] for k in range(8)]
        right = [near_ref[b, k] for k in range(9)]
        acc_x = jnp.zeros((CAP, NZ * CAP), jnp.float32)
        acc_y = acc_x
        acc_z = acc_x
        for step in range(-2, 3):
            xj, yj, zj, uj, vj, wj, mj, rj, pj = [shifted(r, step) for r in right]
            dx = left[0] - xj
            dy = left[1] - yj
            dz = left[2] - zj
            dist_sq = dx * dx + dy * dy + dz * dz
            radius = jnp.sqrt(dist_sq)
            falloff = jnp.maximum(1.0 - 0.5 * radius, 0.0)
            slope_coef = 5.0 * kernel_norm * (falloff * falloff * falloff)
            vel_dot = (left[3] - uj) * dx + (left[4] - vj) * dy + (left[5] - wj) * dz
            viscous = (-visc_alpha * sound_speed) * jnp.minimum(vel_dot, 0.0) / (
                (dist_sq + eta_square) * (0.5 * (left[6] + rj))
            )
            pair_coef = mj * (left[7] + pj + viscous) * slope_coef
            acc_x = acc_x + pair_coef * dx
            acc_y = acc_y + pair_coef * dy
            acc_z = acc_z + pair_coef * dz
        return [acc_x, acc_y, acc_z]

    pair_loop(first_ref, second_ref, count_ref, near_ref.shape[0] - 1, contribution, out_ref, 32)


def pair_pass(kernel, first_ids, second_ids, pair_count, own_rows, near_rows, out_depth):
    pencils = own_rows.shape[0]
    out_shape = (pencils, out_depth, CAP, NZ * CAP)
    vmem = pl.BlockSpec(memory_space=pltpu.VMEM)
    return pl.pallas_call(
        kernel,
        out_shape=jax.ShapeDtypeStruct(out_shape, jnp.float32),
        grid_spec=pltpu.PrefetchScalarGridSpec(
            num_scalar_prefetch=3,
            grid=(1,),
            in_specs=[vmem, vmem],
            out_specs=vmem,
        ),
    )(first_ids, second_ids, pair_count.reshape(1), own_rows, near_rows)


def with_dummy(values_in):
    return jnp.concatenate(
        [values_in, jnp.zeros((values_in.shape[0], 1, values_in.shape[2]), values_in.dtype)], axis=1
    )


def guarded(density, masses):
    return jnp.where(masses > 0.0, density, rest_density)


HIGHEST = lax.Precision.HIGHEST


def window_maps(counts, starts, capacity, row_count):
    lanes_total = counts.shape[0]
    span = (127 + capacity + 127) // 128
    chunk_total = (row_count + 127) // 128 + span
    first_chunk = starts // 128
    offset = starts % 128
    k = jnp.arange(span * 128, dtype=jnp.int32)
    w = jnp.arange(capacity, dtype=jnp.int32)
    shift_map = (
        (k[None, :, None] == offset[:, None, None] + w[None, None, :])
        & (w[None, None, :] < counts[:, None, None])
    ).astype(jnp.float32)
    t = jnp.arange(chunk_total, dtype=jnp.int32)
    chunk_map = (
        t[None, None, :] == first_chunk[:, None, None] + jnp.arange(span, dtype=jnp.int32)[None, :, None]
    ).astype(jnp.float32).reshape(lanes_total * span, chunk_total)
    return shift_map, chunk_map, chunk_total


def local(particles, routing, tile_list):
    lanes_total = lax.axis_size("gx")
    row_count = particles.shape[2]
    capacity = 2 * row_count // lanes_total
    pencil_slots = NZ * CAP
    pencils = CX * CY
    slots_all = pencils * pencil_slots
    ext_count = (CX + 4) * (CY + 4)
    fields = particles[0]
    owner_of = routing[0, 0]
    slot_ids = routing[0, 1]
    owner_ids = jnp.arange(lanes_total, dtype=jnp.int32)
    match_owner = owner_of[None, :] == owner_ids[:, None]
    counts = jnp.sum(match_owner.astype(jnp.int32), axis=1)
    starts = jnp.cumsum(counts) - counts
    within = jnp.arange(capacity, dtype=jnp.int32)
    is_valid = within[None, :] < counts[:, None]
    packed = jnp.concatenate([fields, slot_ids.astype(jnp.float32)[None, :]], axis=0)
    shift_map, chunk_map, chunk_total = window_maps(counts, starts, capacity, row_count)
    chunked = jnp.pad(packed, ((0, 0), (0, chunk_total * 128 - row_count)))
    windows = jnp.einsum(
        "jt,ftl->fjl", chunk_map, chunked.reshape(8, chunk_total, 128), precision=HIGHEST
    ).reshape(8, lanes_total, -1)
    outgoing = jnp.einsum("fok,okw->fow", windows, shift_map, precision=HIGHEST)
    marker = jnp.where(is_valid, outgoing[7], float(slots_all))
    outgoing = jnp.concatenate([outgoing[:7], marker[None]], axis=0)
    arrived = lax.all_to_all(outgoing, "gx", split_axis=1, concat_axis=1, tiled=True)
    arrived_slot = arrived[7].reshape(-1).astype(jnp.int32)
    own_grid = (
        jnp.zeros((7, slots_all), jnp.float32)
        .at[:, arrived_slot]
        .set(arrived[:7].reshape(7, -1), mode="drop")
    )
    own_grid = own_grid.reshape(7, CX, CY, pencil_slots)
    own_flat = own_grid.reshape(7, pencils, pencil_slots)
    mass_own = own_flat[6]
    pos_own = own_flat[0:3]
    first_list = tile_list[0, 0]
    second_list = tile_list[0, 1]
    pair_count = jnp.sum((second_list < ext_count).astype(jnp.int32))
    local_fields = jnp.concatenate([own_grid[0:3], own_grid[6:7]], axis=0)
    near_first = extended(local_fields, (("gx", 1), ("gy", 2)), 2)
    own_pos = jnp.concatenate(
        [pos_own, jnp.zeros((5, pencils, pencil_slots), jnp.float32)], axis=0
    ).transpose(1, 0, 2)
    near_rows = expand_cells(near_first.reshape(4, ext_count, pencil_slots), ext_count)
    density_sums = pair_pass(
        density_kernel, first_list, second_list, pair_count, own_pos, near_rows, 1
    )
    density_own = guarded(jnp.sum(density_sums[:, 0], axis=1), mass_own)
    second_fields = jnp.concatenate(
        [own_grid[3:6], density_own.reshape(1, CX, CY, pencil_slots)], axis=0
    )
    near_second = extended(second_fields, (("gx", 1), ("gy", 2)), 2)
    pos_near = near_first[0:3]
    mass_near = near_first[3]
    vel_near = near_second[0:3]
    density_near = guarded(near_second[3], mass_near)
    pterm_near = pressure_term(density_near)
    rows_b = jnp.concatenate(
        [pos_near, vel_near, mass_near[None], density_near[None], pterm_near[None]], axis=0
    )
    rows_b = expand_cells(rows_b.reshape(9, ext_count, pencil_slots), ext_count)
    rows_a = jnp.concatenate(
        [own_flat[0:6], density_own[None], pressure_term(density_own)[None]], axis=0
    ).transpose(1, 0, 2)
    accel = pair_pass(force_kernel, first_list, second_list, pair_count, rows_a, rows_b, 3)
    accel = jnp.sum(accel, axis=2).transpose(1, 0, 2)
    accel = accel.at[2].add(-gravity)
    results = jnp.concatenate([accel, density_own[None]], axis=0).reshape(4, slots_all)
    reply = jnp.take(results, jnp.minimum(arrived_slot, slots_all - 1), axis=1).reshape(
        4, lanes_total, capacity
    )
    home_rows = lax.all_to_all(reply, "gx", split_axis=1, concat_axis=1, tiled=True)
    spread = jnp.einsum("fow,okw->fok", jnp.where(is_valid[None], home_rows.reshape(4, lanes_total, capacity), 0.0), shift_map, precision=HIGHEST)
    answer = jnp.einsum(
        "jt,fjl->ftl", chunk_map, spread.reshape(4, chunk_map.shape[0], 128), precision=HIGHEST
    ).reshape(4, chunk_total * 128)[:, :row_count]
    return answer[None]


def solution(mesh):
    in_specs = (P("gy", None, "gx"), P("gy", None, "gx"), P("gy", None, "gx"))
    out_specs = P("gy", None, "gx")
    return jax.shard_map(local, mesh=mesh, in_specs=in_specs, out_specs=out_specs, check_vma=False)
```
